512 devices in a mesh: space: 16 (over z_hi, x), inst: 32 (over y, z_lo, core).
Axes of the slice: x: 4, y: 4, z: 16 (z_hi: 4, z_lo: 4; z = z_hi * 4 + z_lo), core: 2. Of those that a mesh axis runs over, the one named last changes fastest.
Arguments:
- flow_state: float32 [32, 7, 65536], P('inst', None, 'space'), may hold values from -5.5 to 5.5
- face_nbr: int32 [6, 65536], P(None, 'space'), may hold values from 0 to 5119
- halo_send: int32 [2, 8192], P(None, 'space'), may hold values from 0 to 4095, as said below
- face_area: float32 [3, 6, 65536], P(None, None, 'space'), may hold values from -3 to 3
- cell_volume: float32 [65536], P(('space', 'inst')), may hold values from 0.5 to 2
- flux_left: float32 [7, 7], replicated, may hold values from -2 to 2
- flux_right: float32 [7, 7], replicated, may hold values from -2 to 2
Outputs:
- inverse: float32 [2, 7, 7, 16, 65536], P(None, None, None, None, ('space', 'inst'))
The draws below stay inside these ranges and needn't reach their ends.
Inputs may be any that keep to these rules, and one draw needn't show every extreme that they name: `halo_send`: within each slab's block of 512 columns, row 0 lists each cell of local indices (7) * 512 to 4095 once and row 1 each cell of local indices 0 to 511 once.
All inputs are finite; a program needn't handle non-finite values.
Results may differ from the reference program's by a relative error of at most 0.0001.
Values sent between devices are 32-bit elements; how exact they have to be, the bound alone decides.
A program may use at most 128 MiB of HBM per device.

```python
import math
import jax
import jax.numpy as jnp
from jax import lax

NVAR = 7
INSTANCES = 32
HARM = 16
FACES = 6
LAYERS = 8
SECTION = 512
CELL_DEV = 4096
NCELL = 65536


def slab_orders(key):
    slab_count = NCELL // CELL_DEV
    subkeys = jax.random.split(jax.random.fold_in(key, 4711), 3)

    def orders(subkey):
        return jax.vmap(lambda inner: jax.random.permutation(inner, SECTION))(jax.random.split(subkey, slab_count)).astype(jnp.int32)
    return (orders(subkeys[0]), orders(subkeys[1]), orders(subkeys[2]))


def draw_halo_send(key, part):
    top_order, bottom_order, cycle_order = slab_orders(key)
    upper_row = (LAYERS - 1) * SECTION + top_order
    return jnp.stack([upper_row.reshape(-1), bottom_order.reshape(-1)]).astype(jnp.int32)


def draw_face_nbr(key, part):
    top_order, bottom_order, cycle_order = slab_orders(key)
    slab_count = NCELL // CELL_DEV
    from_below = jnp.roll(jnp.argsort(top_order, axis=1), 1, axis=0).astype(jnp.int32)
    from_above = jnp.roll(jnp.argsort(bottom_order, axis=1), -1, axis=0).astype(jnp.int32)
    cycle_place = jnp.argsort(cycle_order, axis=1).astype(jnp.int32)
    layer_index = jnp.arange(LAYERS, dtype=jnp.int32)[None, :, None]
    position = jnp.arange(SECTION, dtype=jnp.int32)[None, None, :]
    full_shape = (slab_count, LAYERS, SECTION)
    down_face = jnp.where(layer_index > 0, (layer_index - 1) * SECTION + position, CELL_DEV + from_below[:, None, :])
    up_face = jnp.where(layer_index < LAYERS - 1, (layer_index + 1) * SECTION + position, CELL_DEV + SECTION + from_above[:, None, :])
    listing = [down_face, up_face]
    for offset in (1, -1, 2, -2):
        beside = jnp.take_along_axis(cycle_order, (cycle_place + offset) % SECTION, axis=1)
        listing.append(layer_index * SECTION + beside[:, None, :])
    stacked = jnp.stack([jnp.broadcast_to(face_rows, full_shape) for face_rows in listing])
    return stacked.reshape(6, NCELL).astype(jnp.int32)


def draw_flow_state(key, part):
    subkeys = jax.random.split(jax.random.fold_in(key, 913), 3)
    levels = jnp.array([1.0, 2.0, 1.5, 2.5, 3.0, 1.2, 1.8], dtype=jnp.float32)[:NVAR]
    factor = jax.random.uniform(subkeys[0], (NVAR, NCELL), jnp.float32, 0.5, 1.5)
    coin = jax.random.bernoulli(subkeys[1], 0.5, (NVAR, NCELL))
    variable = jnp.arange(NVAR, dtype=jnp.int32)[:, None]
    signed_rows = (variable >= 1) & (variable <= 3)
    signs = jnp.where(signed_rows & coin, -1.0, 1.0).astype(jnp.float32)
    base_flow = levels[:, None] * factor * signs
    spread = jnp.clip(0.3 * jax.random.normal(subkeys[2], (INSTANCES, NVAR, NCELL), jnp.float32), -1.0, 1.0)
    return (base_flow[None] + spread).astype(jnp.float32)


def steps_of(key, dims, cuts, smallest, high):
    gain = 1.0
    for axis_at, blocks in cuts:
        draws = jax.random.uniform(jax.random.fold_in(jax.random.fold_in(key, 6), axis_at), (blocks,), jnp.float32, smallest / len(cuts), high / len(cuts))
        gain = gain * jnp.repeat(jnp.exp(draws), dims[axis_at] // blocks).reshape((-1,) + (1,) * (len(dims) - 1 - axis_at))
    return gain


def gaussian(own_key, extent, deviation, limit, cuts=(), kind=jnp.bfloat16):
    level = steps_of(own_key, extent, cuts, -0.22, 0.18) if cuts else 1.0
    values = jax.random.normal(own_key, extent, jnp.float32) * deviation * level
    return jnp.minimum(jnp.maximum(values, -limit), limit).astype(kind)


def setup_inputs(seed: int = 0) -> dict:
    keys = jax.random.split(jax.random.key(seed), 8)
    return {
        "flow_state": draw_flow_state(jax.random.fold_in(keys[7], 71), 0),
        "face_nbr": draw_face_nbr(jax.random.fold_in(keys[7], 71), 0),
        "halo_send": draw_halo_send(jax.random.fold_in(keys[7], 71), 0),
        "face_area": gaussian(keys[3], (3, FACES, NCELL), 0.5, 3.0, ((2, 16),), jnp.float32),
        "cell_volume": jnp.clip(jnp.exp(math.log(2.0) - 1.3862944 * jax.random.uniform(keys[4], (NCELL,), jnp.float32) ** steps_of(keys[4], (NCELL,), ((0, 512),), -0.2, 0.2)), 0.5, 2.0),
        "flux_left": gaussian(keys[5], (NVAR, NVAR), NVAR ** -0.5, 2.0, (), jnp.float32),
        "flux_right": gaussian(keys[6], (NVAR, NVAR), NVAR ** -0.5, 2.0, (), jnp.float32),
    }


frequency = 0.1


def face_terms(face_mean, normal_flux, flux_left, flux_right):
    coupling = flux_left[:, :, None] * flux_right[None, :, :]
    jacobian = jnp.einsum("imj,bmc->bijc", coupling, face_mean, precision=lax.Precision.HIGHEST)
    identity = jnp.eye(face_mean.shape[1], dtype=jnp.float32)
    jacobian = jacobian + normal_flux[:, None, None, :] * identity[None, :, :, None]
    spectral = jnp.max(jnp.sum(jnp.abs(jacobian), axis=2), axis=1) + 0.5
    return jnp.sum(0.5 * (jacobian + spectral[:, None, None, :] * identity[None, :, :, None]), axis=0)


def invert(real_part, imag_part):
    size_vars = real_part.shape[0]
    identity = jnp.broadcast_to(jnp.eye(size_vars, dtype=jnp.float32)[:, :, None, None], real_part.shape)
    aug_real = jnp.concatenate([real_part, identity], axis=1)
    aug_imag = jnp.concatenate([imag_part, jnp.zeros_like(identity)], axis=1)
    for column in range(size_vars):
        lead_real = aug_real[column, column]
        lead_imag = aug_imag[column, column]
        inverse_norm = 1.0 / (lead_real * lead_real + lead_imag * lead_imag)
        recip_real = lead_real * inverse_norm
        recip_imag = -lead_imag * inverse_norm
        row_real = aug_real[column] * recip_real - aug_imag[column] * recip_imag
        row_imag = aug_real[column] * recip_imag + aug_imag[column] * recip_real
        col_real = aug_real[:, column:column + 1]
        col_imag = aug_imag[:, column:column + 1]
        aug_real = aug_real - (col_real * row_real[None] - col_imag * row_imag[None])
        aug_imag = aug_imag - (col_real * row_imag[None] + col_imag * row_real[None])
        aug_real = aug_real.at[column].set(row_real)
        aug_imag = aug_imag.at[column].set(row_imag)
    return aug_real[:, size_vars:], aug_imag[:, size_vars:]


def neighbour_cells(face_nbr, halo_send):
    cell_total = face_nbr.shape[1]
    slab_count = cell_total // CELL_DEV
    slab_index = (jnp.arange(cell_total, dtype=jnp.int32) // CELL_DEV)[None, :]
    inside = face_nbr < CELL_DEV
    from_low = face_nbr < CELL_DEV + SECTION
    slot_low = jnp.clip(face_nbr - CELL_DEV, 0, SECTION - 1).astype(jnp.int32)
    slot_high = jnp.clip(face_nbr - CELL_DEV - SECTION, 0, SECTION - 1).astype(jnp.int32)
    below = jnp.clip(slab_index - 1, 0, slab_count - 1).astype(jnp.int32)
    above = jnp.clip(slab_index + 1, 0, slab_count - 1).astype(jnp.int32)
    cell_low = halo_send[0][below * SECTION + slot_low] + below * CELL_DEV
    cell_high = halo_send[1][above * SECTION + slot_high] + above * CELL_DEV
    global_cell = jnp.where(inside, slab_index * CELL_DEV + face_nbr, jnp.where(from_low, cell_low, cell_high)).astype(jnp.int32)
    present = jnp.where(inside, True, jnp.where(from_low, slab_index > 0, slab_index < slab_count - 1))
    return global_cell, present.astype(jnp.float32)


def reference(flow_state, face_nbr, halo_send, face_area, cell_volume, flux_left, flux_right):
    components = flow_state.shape[1]
    cell_total = flow_state.shape[2]
    face_count = face_nbr.shape[0]
    global_cell, present = neighbour_cells(face_nbr, halo_send)

    def one_instance(running, inst_state):
        for direction in range(face_count):
            neighbour = inst_state[:, global_cell[direction]] * present[direction][None, :]
            face_mean = 0.5 * (inst_state + neighbour)
            normals = face_area[:, direction]
            normal_flux = face_mean[1] * normals[0] + face_mean[2] * normals[1] + face_mean[3] * normals[2]
            running = running + face_terms(face_mean[None], normal_flux[None], flux_left, flux_right)
        return running, None

    summed, _ = lax.scan(one_instance, jnp.zeros((components, components, cell_total), jnp.float32), flow_state)
    jacobian_mean = summed / (face_count * INSTANCES)
    blocks = cell_total // CELL_DEV
    mean_blocks = jacobian_mean.reshape(components, components, blocks, CELL_DEV).transpose(2, 0, 1, 3)
    volume_blocks = cell_volume.reshape(blocks, CELL_DEV)
    harmonics = jnp.arange(1, HARM + 1, dtype=jnp.int32).astype(jnp.float32)

    def one_block(pieces):
        block_mean, block_volume = pieces
        imag_shift = harmonics[:, None] * frequency * block_volume[None, :]
        real_part = jnp.broadcast_to(block_mean[:, :, None, :], (components, components, HARM, CELL_DEV))
        imag_part = jnp.eye(components, dtype=jnp.float32)[:, :, None, None] * imag_shift[None, None]
        inv_real, inv_imag = invert(real_part, imag_part)
        return jnp.stack([inv_real, inv_imag])

    result = lax.map(one_block, (mean_blocks, volume_blocks))
    return result.transpose(1, 2, 3, 4, 0, 5).reshape(2, components, components, HARM, cell_total)
```

```python
import functools

import jax
import jax.numpy as jnp
from jax import lax
from jax.experimental import pallas as pl
from jax.experimental.pallas import tpu as pltpu
from jax.sharding import PartitionSpec as P

INSTANCES = 32
HARM = 16
NVAR = 7
FACES = 6
LANES = 128

frequency = 0.1


def lane_gather(rows, lane):
    return jnp.take_along_axis(rows, lane, axis=1, mode="promise_in_bounds")


def wide(row):
    return jnp.broadcast_to(row, (8, LANES))


def sums_kernel(
    slabs, owners,
    state, nbr, send, area, left, right,
    out,
    idx, areas, halo_idx, up, down, from_low, from_high, nb, coupling, outbox, inbox,
    halo_send_sem, halo_recv_sem, send_sem, recv_sem,
):
    space = lax.axis_index("space")
    inst = lax.axis_index("inst")
    above = lax.rem(space + 1, slabs)
    below = lax.rem(space + slabs - 1, slabs)

    barrier = pltpu.get_barrier_semaphore()
    pl.semaphore_signal(barrier, inc=1, device_id={"space": above}, device_id_type=pl.DeviceIdType.MESH)
    pl.semaphore_signal(barrier, inc=1, device_id={"space": below}, device_id_type=pl.DeviceIdType.MESH)

    def greet(step, carry):
        other = lax.rem(inst + step, owners)
        pl.semaphore_signal(barrier, inc=1, device_id={"inst": other}, device_id_type=pl.DeviceIdType.MESH)
        return carry

    lax.fori_loop(1, owners, greet, 0)

    for k in range(4):
        halo_idx[pl.ds(k, 1)] = send[0:1, LANES * k : LANES * (k + 1)]
        halo_idx[pl.ds(4 + k, 1)] = send[1:2, LANES * k : LANES * (k + 1)]
    hidx = halo_idx[...]
    hlane = hidx & (LANES - 1)
    hrow = (hidx >> 7) & 3
    upper = lax.broadcasted_iota(jnp.int32, (8, LANES), 0) < 4
    for c in range(NVAR):
        found = jnp.zeros((8, LANES), jnp.float32)
        for q in range(4):
            rows = jnp.where(upper, wide(state[c, pl.ds(28 + q, 1)]), wide(state[c, pl.ds(q, 1)]))
            found = jnp.where(hrow == q, lane_gather(rows, hlane), found)
        up[pl.ds(4 * c, 4)] = found[0:4]
        down[pl.ds(4 * c, 4)] = found[4:8]

    def regroup(k, carry):
        q = k // 8
        s = lax.rem(k, 8)
        col = pl.multiple_of(k * LANES, LANES)
        idx[pl.ds(q * 48 + s, FACES, stride=8)] = nbr[:, pl.ds(col, LANES)]
        for x in range(3):
            areas[x, pl.ds(q * 48 + s, FACES, stride=8)] = area[x, :, pl.ds(col, LANES)]
        return carry

    lax.fori_loop(0, 32, regroup, 0)

    for i in range(NVAR):
        for m in range(NVAR):
            for j in range(NVAR):
                coupling[(i * NVAR + m) * NVAR + j] = jnp.full((8, LANES), left[i, m] * right[m, j], jnp.float32)

    pl.semaphore_wait(barrier, owners + 1)
    rise = pltpu.make_async_remote_copy(
        src_ref=up, dst_ref=from_low, send_sem=halo_send_sem.at[0], recv_sem=halo_recv_sem.at[0],
        device_id={"space": above}, device_id_type=pl.DeviceIdType.MESH,
    )
    sink = pltpu.make_async_remote_copy(
        src_ref=down, dst_ref=from_high, send_sem=halo_send_sem.at[1], recv_sem=halo_recv_sem.at[1],
        device_id={"space": below}, device_id_type=pl.DeviceIdType.MESH,
    )
    rise.start()
    sink.start()

    def local(g, carry):
        cells = idx[pl.ds(pl.multiple_of(g * 8, 8), 8)]
        lane = cells & (LANES - 1)
        row = cells >> 7
        found = [jnp.zeros((8, LANES), jnp.float32) for _ in range(NVAR)]
        for r in range(32):
            here = row == r
            for c in range(NVAR):
                found[c] = jnp.where(here, lane_gather(wide(state[c, pl.ds(r, 1)]), lane), found[c])
        for c in range(NVAR):
            nb[g, c] = found[c]
        return carry

    lax.fori_loop(0, 4 * FACES, local, 0)

    rise.wait()
    sink.wait()
    from_low[...] = jnp.where(space > 0, from_low[...], 0.0)
    from_high[...] = jnp.where(space < slabs - 1, from_high[...], 0.0)

    def group(q, carry):
        first = pl.multiple_of(q * 8, 8)

        def face(d, totals):
            g = q * FACES + d
            at = pl.multiple_of(g * 8, 8)
            cells = idx[pl.ds(at, 8)]
            lane = cells & (LANES - 1)
            row = cells >> 7
            found = [nb[g, c] for c in range(NVAR)]
            for r in range(8):
                here = row == 32 + r
                source = from_low if r < 4 else from_high
                for c in range(NVAR):
                    line = source[pl.ds(4 * c + r % 4, 1)]
                    found[c] = jnp.where(here, lane_gather(wide(line), lane), found[c])
            mean = [0.5 * (state[c, pl.ds(first, 8)] + found[c]) for c in range(NVAR)]
            flux = (
                mean[1] * areas[0, pl.ds(at, 8)]
                + mean[2] * areas[1, pl.ds(at, 8)]
                + mean[3] * areas[2, pl.ds(at, 8)]
            )
            largest = None
            for i in range(NVAR):
                row_sum = None
                for j in range(NVAR):
                    entry = flux if i == j else None
                    for m in range(NVAR):
                        term = coupling[(i * NVAR + m) * NVAR + j] * mean[m]
                        entry = term if entry is None else entry + term
                    entry = jnp.abs(entry)
                    row_sum = entry if row_sum is None else row_sum + entry
                largest = row_sum if largest is None else jnp.maximum(largest, row_sum)
            last = flux + (largest + 0.5)
            return tuple(t + x for t, x in zip(totals, mean + [last]))

        totals = lax.fori_loop(0, FACES, face, tuple(jnp.zeros((8, LANES), jnp.float32) for _ in range(8)))
        for c in range(8):
            outbox[pl.ds(q * 64 + c, 8, stride=8)] = totals[c]

        def post(k, carry):
            owner = q * 8 + k

            @pl.when(owner != inst)
            def _():
                slot = lax.rem(inst - owner + owners, owners) - 1
                pltpu.make_async_remote_copy(
                    src_ref=outbox.at[pl.ds(pl.multiple_of(owner * 8, 8), 8)],
                    dst_ref=inbox.at[pl.ds(pl.multiple_of(slot * 8, 8), 8)],
                    send_sem=send_sem, recv_sem=recv_sem,
                    device_id={"inst": owner}, device_id_type=pl.DeviceIdType.MESH,
                ).start()

            return carry

        lax.fori_loop(0, 8, post, 0)
        return carry

    lax.fori_loop(0, 4, group, 0)
    pltpu.make_async_copy(inbox, inbox, recv_sem).wait()
    total = outbox[pl.ds(pl.multiple_of(inst * 8, 8), 8)]
    for k in range(31):
        total = total + inbox[8 * k : 8 * k + 8]
    out[...] = total
    pltpu.make_async_copy(inbox, inbox, send_sem).wait()


def invert_kernel(sums, volume, left, right, out):
    scale = 1.0 / (2.0 * FACES * INSTANCES)
    part = [jnp.broadcast_to(sums[pl.ds(m, 1)], (8, LANES)) for m in range(NVAR + 1)]
    harmonic = lax.broadcasted_iota(jnp.int32, (HARM, LANES), 0).astype(jnp.float32) + 1.0
    shift = harmonic * frequency * jnp.broadcast_to(volume[...], (HARM, LANES))
    real = {}
    imag = {}
    for i in range(NVAR):
        for j in range(NVAR):
            entry = part[NVAR] if i == j else None
            for m in range(NVAR):
                term = (left[i, m] * right[m, j]) * part[m]
                entry = term if entry is None else entry + term
            entry = entry * scale
            real[i, j] = jnp.concatenate([entry, entry], axis=0)
            imag[i, j] = shift if i == j else None

    def product(ar, ai, br, bi):
        if ai is None and bi is None:
            return ar * br, None
        if ai is None:
            return ar * br, ar * bi
        if bi is None:
            return ar * br, ai * br
        return ar * br - ai * bi, ar * bi + ai * br

    for k in range(NVAR):
        pr, pi = real[k, k], imag[k, k]
        norm = 1.0 / (pr * pr + pi * pi)
        pr, pi = pr * norm, -pi * norm
        for j in range(NVAR):
            if j != k:
                real[k, j], imag[k, j] = product(real[k, j], imag[k, j], pr, pi)
        real[k, k], imag[k, k] = pr, pi
        for i in range(NVAR):
            if i == k:
                continue
            fr, fi = real[i, k], imag[i, k]
            for j in range(NVAR):
                if j == k:
                    continue
                xr, xi = product(fr, fi, real[k, j], imag[k, j])
                real[i, j] = real[i, j] - xr
                if xi is not None:
                    imag[i, j] = -xi if imag[i, j] is None else imag[i, j] - xi
            xr, xi = product(fr, fi, pr, pi)
            real[i, k], imag[i, k] = -xr, -xi
    for i in range(NVAR):
        for j in range(NVAR):
            out[0, i, j] = real[i, j]
            out[1, i, j] = imag[i, j]


def per_device(flow_state, face_nbr, halo_send, face_area, cell_volume, flux_left, flux_right):
    slabs = lax.axis_size("space")
    owners = lax.axis_size("inst")
    share = cell_volume.shape[0]
    state = flow_state.reshape(NVAR, 32, LANES)
    vmem = pl.BlockSpec(memory_space=pltpu.VMEM)
    smem = pl.BlockSpec(memory_space=pltpu.SMEM)
    f32 = jnp.float32
    sums = pl.pallas_call(
        functools.partial(sums_kernel, slabs, owners),
        out_shape=jax.ShapeDtypeStruct((8, LANES), f32),
        in_specs=[vmem, vmem, vmem, vmem, smem, smem],
        out_specs=vmem,
        scratch_shapes=[
            pltpu.VMEM((192, LANES), jnp.int32),
            pltpu.VMEM((3, 192, LANES), f32),
            pltpu.VMEM((8, LANES), jnp.int32),
            pltpu.VMEM((28, LANES), f32),
            pltpu.VMEM((28, LANES), f32),
            pltpu.VMEM((28, LANES), f32),
            pltpu.VMEM((28, LANES), f32),
            pltpu.VMEM((24, NVAR, 8, LANES), f32),
            pltpu.VMEM((343, 8, LANES), f32),
            pltpu.VMEM((256, LANES), f32),
            pltpu.VMEM((248, LANES), f32),
            pltpu.SemaphoreType.DMA((2,)),
            pltpu.SemaphoreType.DMA((2,)),
            pltpu.SemaphoreType.DMA,
            pltpu.SemaphoreType.DMA,
        ],
        compiler_params=pltpu.CompilerParams(collective_id=0, has_side_effects=True),
        name="sums",
    )(state, face_nbr, halo_send, face_area, flux_left, flux_right)
    return pl.pallas_call(
        invert_kernel,
        out_shape=jax.ShapeDtypeStruct((2, NVAR, NVAR, HARM, share), f32),
        in_specs=[vmem, vmem, smem, smem],
        out_specs=vmem,
        name="invert",
    )(sums, cell_volume.reshape(1, share), flux_left, flux_right)


def solution(mesh):
    placed = (
        P("inst", None, "space"),
        P(None, "space"),
        P(None, "space"),
        P(None, None, "space"),
        P(("space", "inst")),
        P(),
        P(),
    )
    return jax.shard_map(
        per_device,
        mesh=mesh,
        in_specs=placed,
        out_specs=P(None, None, None, None, ("space", "inst")),
        check_vma=False,
    )
```

```python
import functools

import jax
import jax.numpy as jnp
from jax import lax
from jax.experimental import pallas as pl
from jax.experimental.pallas import tpu as pltpu
from jax.sharding import PartitionSpec as P

INSTANCES = 32
HARM = 16
NVAR = 7
FACES = 6
LANES = 128

frequency = 0.1


def lane_gather(rows, lane):
    return jnp.take_along_axis(rows, lane, axis=1, mode="promise_in_bounds")


def wide(row):
    return jnp.broadcast_to(row, (8, LANES))


def bits_select(rows, index, bits):
    for b in range(bits):
        odd = ((index >> b) & 1) == 1
        rows = [jnp.where(odd, rows[k + 1], rows[k]) for k in range(0, len(rows), 2)]
    return rows[0]


def two_parts(value):
    high = value.astype(jnp.bfloat16).astype(jnp.float32)
    return high, (value - high).astype(jnp.bfloat16).astype(jnp.float32)


def sums_kernel(
    slabs, owners,
    state_hbm, nbr_hbm, send_hbm, area_hbm, left_hbm, right_hbm,
    out,
    state, nbr, send, area, left, right,
    idx, areas, halo_idx, up, down, from_low, from_high, table_rows, table, factors, weights,
    near, work, outbox, inbox,
    in_sem, halo_send_sem, halo_recv_sem, send_sem, recv_sem,
):
    space = lax.axis_index("space")
    inst = lax.axis_index("inst")
    above = lax.rem(space + 1, slabs)
    below = lax.rem(space + slabs - 1, slabs)
    f32 = jnp.float32
    bf16 = jnp.bfloat16

    loads = [
        pltpu.make_async_copy(src, dst, in_sem.at[k])
        for k, (src, dst) in enumerate(
            [(state_hbm, state), (send_hbm, send), (nbr_hbm, nbr), (left_hbm, left), (right_hbm, right), (area_hbm, area)]
        )
    ]
    for load in loads:
        load.start()

    barrier = pltpu.get_barrier_semaphore()
    pl.semaphore_signal(barrier, inc=1, device_id={"space": above}, device_id_type=pl.DeviceIdType.MESH)
    pl.semaphore_signal(barrier, inc=1, device_id={"space": below}, device_id_type=pl.DeviceIdType.MESH)

    def greet(step, carry):
        other = lax.rem(inst + step, owners)
        pl.semaphore_signal(barrier, inc=1, device_id={"inst": other}, device_id_type=pl.DeviceIdType.MESH)
        return carry

    lax.fori_loop(1, owners, greet, 0)

    loads[0].wait()
    loads[1].wait()
    for k in range(4):
        halo_idx[pl.ds(k, 1)] = send[0:1, LANES * k : LANES * (k + 1)]
        halo_idx[pl.ds(4 + k, 1)] = send[1:2, LANES * k : LANES * (k + 1)]
    hidx = halo_idx[...]
    hlane = hidx & (LANES - 1)
    hrow = (hidx >> 7) & 3
    upper = lax.broadcasted_iota(jnp.int32, (8, LANES), 0) < 4
    for c in range(NVAR):
        found = jnp.zeros((8, LANES), f32)
        for q in range(4):
            rows = jnp.where(upper, wide(state[c, pl.ds(28 + q, 1)]), wide(state[c, pl.ds(q, 1)]))
            found = jnp.where(hrow == q, lane_gather(rows, hlane), found)
        up[pl.ds(4 * c, 4)] = found[0:4]
        down[pl.ds(4 * c, 4)] = found[4:8]

    pl.semaphore_wait(barrier, owners + 1)
    rise = pltpu.make_async_remote_copy(
        src_ref=up, dst_ref=from_low, send_sem=halo_send_sem.at[0], recv_sem=halo_recv_sem.at[0],
        device_id={"space": above}, device_id_type=pl.DeviceIdType.MESH,
    )
    sink = pltpu.make_async_remote_copy(
        src_ref=down, dst_ref=from_high, send_sem=halo_send_sem.at[1], recv_sem=halo_recv_sem.at[1],
        device_id={"space": below}, device_id_type=pl.DeviceIdType.MESH,
    )
    rise.start()
    sink.start()

    for c in range(NVAR):
        table_rows[pl.ds(c, 32, stride=8)] = state[c]
    table_rows[pl.ds(NVAR, 32, stride=8)] = jnp.zeros((32, LANES), f32)
    high, rest = two_parts(table_rows[...])
    table[:, 0:LANES] = high.astype(bf16)
    table[:, LANES : 2 * LANES] = rest.astype(bf16)

    loads[2].wait()

    def regroup(k, carry):
        q = k // 8
        s = lax.rem(k, 8)
        col = pl.multiple_of(k * LANES, LANES)
        idx[pl.ds(q * 48 + s, FACES, stride=8)] = nbr[:, pl.ds(col, LANES)]
        return carry

    lax.fori_loop(0, 32, regroup, 0, unroll=8)

    def by_lanes(g):
        cells = idx[pl.ds(pl.multiple_of(g * 8, 8), 8)]
        lane = cells & (LANES - 1)
        row = cells >> 7
        found = [jnp.zeros((8, LANES), f32) for _ in range(NVAR)]
        for r in range(32):
            here = row == r
            for c in range(NVAR):
                found[c] = jnp.where(here, lane_gather(wide(state[c, pl.ds(r, 1)]), lane), found[c])
        for c in range(NVAR):
            near[pl.ds(g * 64 + c, 8, stride=8)] = found[c]

    position = lax.broadcasted_iota(jnp.int32, (LANES, LANES), 0).astype(f32).astype(bf16)

    def by_matrix(g):
        lines = [idx[pl.ds(g * 8 + a, 1)] for a in range(8)]
        chosen = []
        for line in lines:
            lane = jnp.broadcast_to((line & (LANES - 1)).astype(f32).astype(bf16), (LANES, LANES))
            one = jnp.where(position == lane, bf16(1), bf16(0))
            chosen.append(jnp.concatenate([one, one], axis=0))
        picked = jnp.dot(table[...], jnp.concatenate(chosen, axis=1), preferred_element_type=f32)
        for a in range(8):
            rows = [picked[8 * r : 8 * r + 8, LANES * a : LANES * (a + 1)] for r in range(32)]
            near[pl.ds(pl.multiple_of((g * 8 + a) * 8, 8), 8)] = bits_select(rows, wide(lines[a] >> 7), 5)

    def local(q, carry):
        for d in range(FACES):
            if d < 2:
                by_lanes(q * FACES + d)
            else:
                by_matrix(q * FACES + d)
        return carry

    lax.fori_loop(0, 4, local, 0)

    loads[3].wait()
    loads[4].wait()
    factors[...] = jnp.zeros_like(factors)
    factors[0:NVAR, 0:NVAR] = left[...]
    factors[8 : 8 + NVAR, 0:NVAR] = right[...]
    eye = (
        lax.broadcasted_iota(jnp.int32, (8, LANES), 0) == lax.broadcasted_iota(jnp.int32, (8, LANES), 1)
    ).astype(f32)
    turned = lax.dot_general(
        eye, jnp.concatenate([factors[8:16], jnp.zeros((120, LANES), f32)], axis=0),
        (((1,), (1,)), ((), ())), precision=lax.Precision.HIGHEST, preferred_element_type=f32,
    )
    lane_at = lax.broadcasted_iota(jnp.int32, (8, LANES), 1)
    row_at = lax.broadcasted_iota(jnp.int32, (8, LANES), 0)
    for j in range(NVAR):
        line = factors[0:8] * wide(turned[j : j + 1])
        line = jnp.where((lane_at == NVAR) & (row_at == j), 1.0, line)
        high, rest = two_parts(line)
        packed = high + pltpu.roll(high, 8, 1) + pltpu.roll(rest, 16, 1) + pltpu.roll(rest, 24, 1)
        weights[8 * j : 8 * j + 8] = packed.astype(bf16)

    loads[5].wait()

    def regroup_area(k, carry):
        q = k // 8
        s = lax.rem(k, 8)
        col = pl.multiple_of(k * LANES, LANES)
        for x in range(3):
            areas[x, pl.ds(q * 48 + s, FACES, stride=8)] = area[x, :, pl.ds(col, LANES)]
        return carry

    lax.fori_loop(0, 32, regroup_area, 0, unroll=8)

    rise.wait()
    sink.wait()
    from_low[...] = jnp.where(space > 0, from_low[...], 0.0)
    from_high[...] = jnp.where(space < slabs - 1, from_high[...], 0.0)

    def group(q, carry):
        first = pl.multiple_of(q * 8, 8)
        totals = [jnp.zeros((8, LANES), f32) for _ in range(8)]
        for d in range(FACES):
            g = q * FACES + d
            at = pl.multiple_of(g * 8, 8)
            cells = idx[pl.ds(at, 8)]
            lane = cells & (LANES - 1)
            row = cells >> 7
            found = [near[pl.ds(g * 64 + c, 8, stride=8)] for c in range(NVAR)]
            for r in range(8):
                here = row == 32 + r
                source = from_low if r < 4 else from_high
                for c in range(NVAR):
                    line = source[pl.ds(4 * c + r % 4, 1)]
                    found[c] = jnp.where(here, lane_gather(wide(line), lane), found[c])
            mean = [0.5 * (state[c, pl.ds(first, 8)] + found[c]) for c in range(NVAR)]
            flux = (
                mean[1] * areas[0, pl.ds(at, 8)]
                + mean[2] * areas[1, pl.ds(at, 8)]
                + mean[3] * areas[2, pl.ds(at, 8)]
            )
            for c in range(8):
                work[d, pl.ds(c, 8, stride=8)] = mean[c] if c < NVAR else flux
            columns = []
            for a in range(8):
                high, rest = two_parts(work[d, 8 * a : 8 * a + 8])
                columns.append(jnp.concatenate([high, rest, high, rest], axis=0).astype(bf16))
            entries = jnp.dot(weights[:, 0:32], jnp.concatenate(columns, axis=1), preferred_element_type=f32)
            for a in range(8):
                row_sum = None
                for j in range(NVAR):
                    entry = jnp.abs(entries[8 * j : 8 * j + 8, LANES * a : LANES * (a + 1)])
                    row_sum = entry if row_sum is None else row_sum + entry
                work[d, 8 * a : 8 * a + 8] = row_sum
            largest = work[d, pl.ds(0, 8, stride=8)]
            for i in range(1, NVAR):
                largest = jnp.maximum(largest, work[d, pl.ds(i, 8, stride=8)])
            last = flux + (largest + 0.5)
            totals = [t + x for t, x in zip(totals, mean + [last])]
        for c in range(8):
            outbox[pl.ds(q * 64 + c, 8, stride=8)] = totals[c]

        def post(k, carry):
            owner = q * 8 + k

            @pl.when(owner != inst)
            def _():
                slot = lax.rem(inst - owner + owners, owners) - 1
                pltpu.make_async_remote_copy(
                    src_ref=outbox.at[pl.ds(pl.multiple_of(owner * 8, 8), 8)],
                    dst_ref=inbox.at[pl.ds(pl.multiple_of(slot * 8, 8), 8)],
                    send_sem=send_sem, recv_sem=recv_sem,
                    device_id={"inst": owner}, device_id_type=pl.DeviceIdType.MESH,
                ).start()

            return carry

        lax.fori_loop(0, 8, post, 0)
        return carry

    lax.fori_loop(0, 4, group, 0)
    pltpu.make_async_copy(inbox, inbox, recv_sem).wait()
    total = outbox[pl.ds(pl.multiple_of(inst * 8, 8), 8)]
    for k in range(31):
        total = total + inbox[8 * k : 8 * k + 8]
    out[...] = total
    pltpu.make_async_copy(inbox, inbox, send_sem).wait()


def invert_kernel(sums, volume, left, right, out):
    scale = 1.0 / (2.0 * FACES * INSTANCES)
    part = [jnp.broadcast_to(sums[pl.ds(m, 1)], (8, LANES)) for m in range(NVAR + 1)]
    harmonic = lax.broadcasted_iota(jnp.int32, (HARM, LANES), 0).astype(jnp.float32) + 1.0
    shift = harmonic * frequency * jnp.broadcast_to(volume[...], (HARM, LANES))
    real = {}
    imag = {}
    for i in range(NVAR):
        for j in range(NVAR):
            entry = part[NVAR] if i == j else None
            for m in range(NVAR):
                term = (left[i, m] * right[m, j]) * part[m]
                entry = term if entry is None else entry + term
            entry = entry * scale
            real[i, j] = jnp.concatenate([entry, entry], axis=0)
            imag[i, j] = shift if i == j else None

    def product(ar, ai, br, bi):
        if ai is None and bi is None:
            return ar * br, None
        if ai is None:
            return ar * br, ar * bi
        if bi is None:
            return ar * br, ai * br
        return ar * br - ai * bi, ar * bi + ai * br

    for k in range(NVAR):
        pr, pi = real[k, k], imag[k, k]
        norm = 1.0 / (pr * pr + pi * pi)
        pr, pi = pr * norm, -pi * norm
        for j in range(NVAR):
            if j != k:
                real[k, j], imag[k, j] = product(real[k, j], imag[k, j], pr, pi)
        real[k, k], imag[k, k] = pr, pi
        for i in range(NVAR):
            if i == k:
                continue
            fr, fi = real[i, k], imag[i, k]
            for j in range(NVAR):
                if j == k:
                    continue
                xr, xi = product(fr, fi, real[k, j], imag[k, j])
                real[i, j] = real[i, j] - xr
                if xi is not None:
                    imag[i, j] = -xi if imag[i, j] is None else imag[i, j] - xi
            xr, xi = product(fr, fi, pr, pi)
            real[i, k], imag[i, k] = -xr, -xi
    for i in range(NVAR):
        for j in range(NVAR):
            out[0, i, j] = real[i, j]
            out[1, i, j] = imag[i, j]


def per_device(flow_state, face_nbr, halo_send, face_area, cell_volume, flux_left, flux_right):
    slabs = lax.axis_size("space")
    owners = lax.axis_size("inst")
    share = cell_volume.shape[0]
    state = flow_state.reshape(NVAR, 32, LANES)
    vmem = pl.BlockSpec(memory_space=pltpu.VMEM)
    smem = pl.BlockSpec(memory_space=pltpu.SMEM)
    f32 = jnp.float32
    sums = pl.pallas_call(
        functools.partial(sums_kernel, slabs, owners),
        out_shape=jax.ShapeDtypeStruct((8, LANES), f32),
        in_specs=[pl.BlockSpec(memory_space=pl.ANY)] * 6,
        out_specs=vmem,
        scratch_shapes=[
            pltpu.VMEM((NVAR, 32, LANES), f32),
            pltpu.VMEM(face_nbr.shape, jnp.int32),
            pltpu.VMEM(halo_send.shape, jnp.int32),
            pltpu.VMEM(face_area.shape, f32),
            pltpu.VMEM((NVAR, NVAR), f32),
            pltpu.VMEM((NVAR, NVAR), f32),
            pltpu.VMEM((192, LANES), jnp.int32),
            pltpu.VMEM((3, 192, LANES), f32),
            pltpu.VMEM((8, LANES), jnp.int32),
            pltpu.VMEM((28, LANES), f32),
            pltpu.VMEM((28, LANES), f32),
            pltpu.VMEM((28, LANES), f32),
            pltpu.VMEM((28, LANES), f32),
            pltpu.VMEM((256, LANES), f32),
            pltpu.VMEM((256, 2 * LANES), jnp.bfloat16),
            pltpu.VMEM((16, LANES), f32),
            pltpu.VMEM((56, LANES), jnp.bfloat16),
            pltpu.VMEM((1536, LANES), f32),
            pltpu.VMEM((FACES, 64, LANES), f32),
            pltpu.VMEM((256, LANES), f32),
            pltpu.VMEM((248, LANES), f32),
            pltpu.SemaphoreType.DMA((6,)),
            pltpu.SemaphoreType.DMA((2,)),
            pltpu.SemaphoreType.DMA((2,)),
            pltpu.SemaphoreType.DMA,
            pltpu.SemaphoreType.DMA,
        ],
        compiler_params=pltpu.CompilerParams(collective_id=0, has_side_effects=True, vmem_limit_bytes=48 << 20),
        name="sums",
    )(state, face_nbr, halo_send, face_area, flux_left, flux_right)
    return pl.pallas_call(
        invert_kernel,
        out_shape=jax.ShapeDtypeStruct((2, NVAR, NVAR, HARM, share), f32),
        in_specs=[vmem, vmem, smem, smem],
        out_specs=vmem,
        name="invert",
    )(sums, cell_volume.reshape(1, share), flux_left, flux_right)


def solution(mesh):
    placed = (
        P("inst", None, "space"),
        P(None, "space"),
        P(None, "space"),
        P(None, None, "space"),
        P(("space", "inst")),
        P(),
        P(),
    )
    return jax.shard_map(
        per_device,
        mesh=mesh,
        in_specs=placed,
        out_specs=P(None, None, None, None, ("space", "inst")),
        check_vma=False,
    )
```

```python
import functools

import jax
import jax.numpy as jnp
from jax import lax
from jax.experimental import pallas as pl
from jax.experimental.pallas import tpu as pltpu
from jax.sharding import PartitionSpec as P

INSTANCES = 32
HARM = 16
NVAR = 7
FACES = 6
LANES = 128

frequency = 0.1


def lane_gather(rows, lane):
    return jnp.take_along_axis(rows, lane, axis=1, mode="promise_in_bounds")


def wide(row):
    return jnp.broadcast_to(row, (8, LANES))


def bits_select(rows, index, bits):
    for b in range(bits):
        odd = ((index >> b) & 1) == 1
        rows = [jnp.where(odd, rows[k + 1], rows[k]) for k in range(0, len(rows), 2)]
    return rows[0]


def two_parts(value):
    high = value.astype(jnp.bfloat16).astype(jnp.float32)
    return high, (value - high).astype(jnp.bfloat16).astype(jnp.float32)


def sums_kernel(
    slabs, owners,
    state_hbm, nbr_hbm, send_hbm, area_hbm, left_hbm, right_hbm,
    out,
    state, nbr, send, area, left, right,
    idx, areas, halo_idx, up, down, from_low, from_high, table_rows, table, factors, weights,
    near, work, outbox, inbox,
    in_sem, halo_send_sem, halo_recv_sem, send_sem, recv_sem,
):
    space = lax.axis_index("space")
    inst = lax.axis_index("inst")
    above = lax.rem(space + 1, slabs)
    below = lax.rem(space + slabs - 1, slabs)
    f32 = jnp.float32
    bf16 = jnp.bfloat16

    loads = [
        pltpu.make_async_copy(src, dst, in_sem.at[k])
        for k, (src, dst) in enumerate(
            [(state_hbm, state), (send_hbm, send), (nbr_hbm, nbr), (left_hbm, left), (right_hbm, right), (area_hbm, area)]
        )
    ]
    for load in loads:
        load.start()

    barrier = pltpu.get_barrier_semaphore()
    pl.semaphore_signal(barrier, inc=1, device_id={"space": above}, device_id_type=pl.DeviceIdType.MESH)
    pl.semaphore_signal(barrier, inc=1, device_id={"space": below}, device_id_type=pl.DeviceIdType.MESH)

    def greet(step, carry):
        other = lax.rem(inst + step, owners)
        pl.semaphore_signal(barrier, inc=1, device_id={"inst": other}, device_id_type=pl.DeviceIdType.MESH)
        return carry

    lax.fori_loop(1, owners, greet, 0)

    loads[0].wait()
    loads[1].wait()
    for k in range(4):
        halo_idx[pl.ds(k, 1)] = send[0:1, LANES * k : LANES * (k + 1)]
        halo_idx[pl.ds(4 + k, 1)] = send[1:2, LANES * k : LANES * (k + 1)]
    hidx = halo_idx[...]
    hlane = hidx & (LANES - 1)
    hrow = (hidx >> 7) & 3
    upper = lax.broadcasted_iota(jnp.int32, (8, LANES), 0) < 4
    for c in range(NVAR):
        found = jnp.zeros((8, LANES), f32)
        for q in range(4):
            rows = jnp.where(upper, wide(state[c, pl.ds(28 + q, 1)]), wide(state[c, pl.ds(q, 1)]))
            found = jnp.where(hrow == q, lane_gather(rows, hlane), found)
        up[pl.ds(4 * c, 4)] = found[0:4]
        down[pl.ds(4 * c, 4)] = found[4:8]

    pl.semaphore_wait(barrier, owners + 1)
    rise = pltpu.make_async_remote_copy(
        src_ref=up, dst_ref=from_low, send_sem=halo_send_sem.at[0], recv_sem=halo_recv_sem.at[0],
        device_id={"space": above}, device_id_type=pl.DeviceIdType.MESH,
    )
    sink = pltpu.make_async_remote_copy(
        src_ref=down, dst_ref=from_high, send_sem=halo_send_sem.at[1], recv_sem=halo_recv_sem.at[1],
        device_id={"space": below}, device_id_type=pl.DeviceIdType.MESH,
    )
    rise.start()
    sink.start()

    for c in range(NVAR):
        table_rows[pl.ds(c, 32, stride=8)] = state[c]
    table_rows[pl.ds(NVAR, 32, stride=8)] = jnp.zeros((32, LANES), f32)
    high, rest = two_parts(table_rows[...])
    table[:, 0:LANES] = high.astype(bf16)
    table[:, LANES : 2 * LANES] = rest.astype(bf16)

    loads[2].wait()

    def regroup(k, carry):
        q = k // 8
        s = lax.rem(k, 8)
        col = pl.multiple_of(k * LANES, LANES)
        idx[pl.ds(q * 48 + s, FACES, stride=8)] = nbr[:, pl.ds(col, LANES)]
        return carry

    lax.fori_loop(0, 32, regroup, 0, unroll=8)

    def by_lanes(g):
        cells = idx[pl.ds(pl.multiple_of(g * 8, 8), 8)]
        lane = cells & (LANES - 1)
        row = cells >> 7
        found = [jnp.zeros((8, LANES), f32) for _ in range(NVAR)]
        for r in range(32):
            here = row == r
            for c in range(NVAR):
                found[c] = jnp.where(here, lane_gather(wide(state[c, pl.ds(r, 1)]), lane), found[c])
        for c in range(NVAR):
            near[pl.ds(g * 64 + c, 8, stride=8)] = found[c]

    position = lax.broadcasted_iota(jnp.int32, (LANES, LANES), 0).astype(f32).astype(bf16)

    def by_matrix(g):
        lines = [idx[pl.ds(g * 8 + a, 1)] for a in range(8)]
        chosen = []
        for line in lines:
            lane = jnp.broadcast_to((line & (LANES - 1)).astype(f32).astype(bf16), (LANES, LANES))
            one = jnp.where(position == lane, bf16(1), bf16(0))
            chosen.append(jnp.concatenate([one, one], axis=0))
        picked = jnp.dot(table[...], jnp.concatenate(chosen, axis=1), preferred_element_type=f32)
        for a in range(8):
            rows = [picked[8 * r : 8 * r + 8, LANES * a : LANES * (a + 1)] for r in range(32)]
            near[pl.ds(pl.multiple_of((g * 8 + a) * 8, 8), 8)] = bits_select(rows, wide(lines[a] >> 7), 5)

    def local(q, carry):
        for d in range(FACES):
            if d < 2:
                by_lanes(q * FACES + d)
            else:
                by_matrix(q * FACES + d)
        return carry

    lax.fori_loop(0, 4, local, 0)

    loads[3].wait()
    loads[4].wait()
    factors[...] = jnp.zeros_like(factors)
    factors[0:NVAR, 0:NVAR] = left[...]
    factors[8 : 8 + NVAR, 0:NVAR] = right[...]
    eye = (
        lax.broadcasted_iota(jnp.int32, (8, LANES), 0) == lax.broadcasted_iota(jnp.int32, (8, LANES), 1)
    ).astype(f32)
    turned = lax.dot_general(
        eye, jnp.concatenate([factors[8:16], jnp.zeros((120, LANES), f32)], axis=0),
        (((1,), (1,)), ((), ())), precision=lax.Precision.HIGHEST, preferred_element_type=f32,
    )
    lane_at = lax.broadcasted_iota(jnp.int32, (8, LANES), 1)
    row_at = lax.broadcasted_iota(jnp.int32, (8, LANES), 0)
    for j in range(NVAR):
        line = factors[0:8] * wide(turned[j : j + 1])
        line = jnp.where((lane_at == NVAR) & (row_at == j), 1.0, line)
        high, rest = two_parts(line)
        packed = high + pltpu.roll(high, 8, 1) + pltpu.roll(rest, 16, 1) + pltpu.roll(rest, 24, 1)
        weights[8 * j : 8 * j + 8] = packed.astype(bf16)

    loads[5].wait()

    def regroup_area(k, carry):
        q = k // 8
        s = lax.rem(k, 8)
        col = pl.multiple_of(k * LANES, LANES)
        for x in range(3):
            areas[x, pl.ds(q * 48 + s, FACES, stride=8)] = area[x, :, pl.ds(col, LANES)]
        return carry

    lax.fori_loop(0, 32, regroup_area, 0, unroll=8)

    rise.wait()
    sink.wait()
    from_low[...] = jnp.where(space > 0, from_low[...], 0.0)
    from_high[...] = jnp.where(space < slabs - 1, from_high[...], 0.0)

    def group(q, carry):
        first = pl.multiple_of(q * 8, 8)
        totals = [jnp.zeros((8, LANES), f32) for _ in range(8)]
        for d in range(FACES):
            g = q * FACES + d
            at = pl.multiple_of(g * 8, 8)
            cells = idx[pl.ds(at, 8)]
            lane = cells & (LANES - 1)
            row = cells >> 7
            found = [near[pl.ds(g * 64 + c, 8, stride=8)] for c in range(NVAR)]
            for r in range(8):
                here = row == 32 + r
                source = from_low if r < 4 else from_high
                for c in range(NVAR):
                    line = source[pl.ds(4 * c + r % 4, 1)]
                    found[c] = jnp.where(here, lane_gather(wide(line), lane), found[c])
            mean = [0.5 * (state[c, pl.ds(first, 8)] + found[c]) for c in range(NVAR)]
            flux = (
                mean[1] * areas[0, pl.ds(at, 8)]
                + mean[2] * areas[1, pl.ds(at, 8)]
                + mean[3] * areas[2, pl.ds(at, 8)]
            )
            for c in range(8):
                work[d, pl.ds(c, 8, stride=8)] = mean[c] if c < NVAR else flux
            columns = []
            for a in range(8):
                high, rest = two_parts(work[d, 8 * a : 8 * a + 8])
                columns.append(jnp.concatenate([high, rest, high, rest], axis=0).astype(bf16))
            entries = jnp.dot(weights[:, 0:32], jnp.concatenate(columns, axis=1), preferred_element_type=f32)
            for a in range(8):
                row_sum = None
                for j in range(NVAR):
                    entry = jnp.abs(entries[8 * j : 8 * j + 8, LANES * a : LANES * (a + 1)])
                    row_sum = entry if row_sum is None else row_sum + entry
                work[d, 8 * a : 8 * a + 8] = row_sum
            largest = work[d, pl.ds(0, 8, stride=8)]
            for i in range(1, NVAR):
                largest = jnp.maximum(largest, work[d, pl.ds(i, 8, stride=8)])
            last = flux + (largest + 0.5)
            totals = [t + x for t, x in zip(totals, mean + [last])]
        for c in range(8):
            outbox[pl.ds(q * 64 + c, 8, stride=8)] = totals[c]

        def post(k, carry):
            owner = q * 8 + k

            @pl.when(owner != inst)
            def _():
                slot = lax.rem(inst - owner + owners, owners) - 1
                pltpu.make_async_remote_copy(
                    src_ref=outbox.at[pl.ds(pl.multiple_of(owner * 8, 8), 8)],
                    dst_ref=inbox.at[pl.ds(pl.multiple_of(slot * 8, 8), 8)],
                    send_sem=send_sem, recv_sem=recv_sem,
                    device_id={"inst": owner}, device_id_type=pl.DeviceIdType.MESH,
                ).start()

            return carry

        lax.fori_loop(0, 8, post, 0)
        return carry

    lax.fori_loop(0, 4, group, 0)
    pltpu.make_async_copy(inbox, inbox, recv_sem).wait()
    total = outbox[pl.ds(pl.multiple_of(inst * 8, 8), 8)]
    for k in range(31):
        total = total + inbox[8 * k : 8 * k + 8]
    out[...] = total
    pltpu.make_async_copy(inbox, inbox, send_sem).wait()


def invert_kernel(sums, volume, left, right, out):
    scale = 1.0 / (2.0 * FACES * INSTANCES)
    part = [jnp.broadcast_to(sums[pl.ds(m, 1)], (8, LANES)) for m in range(NVAR + 1)]
    harmonic = lax.broadcasted_iota(jnp.int32, (HARM, LANES), 0).astype(jnp.float32) + 1.0
    shift = harmonic * frequency * jnp.broadcast_to(volume[...], (HARM, LANES))
    real = {}
    imag = {}
    for i in range(NVAR):
        for j in range(NVAR):
            entry = part[NVAR] if i == j else None
            for m in range(NVAR):
                term = (left[i, m] * right[m, j]) * part[m]
                entry = term if entry is None else entry + term
            entry = entry * scale
            real[i, j] = jnp.concatenate([entry, entry], axis=0)
            imag[i, j] = shift if i == j else None

    def product(ar, ai, br, bi):
        if ai is None and bi is None:
            return ar * br, None
        if ai is None:
            return ar * br, ar * bi
        if bi is None:
            return ar * br, ai * br
        return ar * br - ai * bi, ar * bi + ai * br

    for k in range(NVAR):
        pr, pi = real[k, k], imag[k, k]
        norm = 1.0 / (pr * pr + pi * pi)
        pr, pi = pr * norm, -pi * norm
        for j in range(NVAR):
            if j != k:
                real[k, j], imag[k, j] = product(real[k, j], imag[k, j], pr, pi)
        real[k, k], imag[k, k] = pr, pi
        for i in range(NVAR):
            if i == k:
                continue
            fr, fi = real[i, k], imag[i, k]
            for j in range(NVAR):
                if j == k:
                    continue
                xr, xi = product(fr, fi, real[k, j], imag[k, j])
                real[i, j] = real[i, j] - xr
                if xi is not None:
                    imag[i, j] = -xi if imag[i, j] is None else imag[i, j] - xi
            xr, xi = product(fr, fi, pr, pi)
            real[i, k], imag[i, k] = -xr, -xi
    for i in range(NVAR):
        for j in range(NVAR):
            out[0, i, j] = real[i, j]
            out[1, i, j] = imag[i, j]


def per_device(flow_state, face_nbr, halo_send, face_area, cell_volume, flux_left, flux_right):
    slabs = lax.axis_size("space")
    owners = lax.axis_size("inst")
    share = cell_volume.shape[0]
    state = flow_state.reshape(NVAR, 32, LANES)
    vmem = pl.BlockSpec(memory_space=pltpu.VMEM)
    smem = pl.BlockSpec(memory_space=pltpu.SMEM)
    f32 = jnp.float32
    sums = pl.pallas_call(
        functools.partial(sums_kernel, slabs, owners),
        out_shape=jax.ShapeDtypeStruct((8, LANES), f32),
        in_specs=[pl.BlockSpec(memory_space=pltpu.HBM)] * 6,
        out_specs=vmem,
        scratch_shapes=[
            pltpu.VMEM((NVAR, 32, LANES), f32),
            pltpu.VMEM(face_nbr.shape, jnp.int32),
            pltpu.VMEM(halo_send.shape, jnp.int32),
            pltpu.VMEM(face_area.shape, f32),
            pltpu.VMEM((NVAR, NVAR), f32),
            pltpu.VMEM((NVAR, NVAR), f32),
            pltpu.VMEM((192, LANES), jnp.int32),
            pltpu.VMEM((3, 192, LANES), f32),
            pltpu.VMEM((8, LANES), jnp.int32),
            pltpu.VMEM((28, LANES), f32),
            pltpu.VMEM((28, LANES), f32),
            pltpu.VMEM((28, LANES), f32),
            pltpu.VMEM((28, LANES), f32),
            pltpu.VMEM((256, LANES), f32),
            pltpu.VMEM((256, 2 * LANES), jnp.bfloat16),
            pltpu.VMEM((16, LANES), f32),
            pltpu.VMEM((56, LANES), jnp.bfloat16),
            pltpu.VMEM((1536, LANES), f32),
            pltpu.VMEM((FACES, 64, LANES), f32),
            pltpu.VMEM((256, LANES), f32),
            pltpu.VMEM((248, LANES), f32),
            pltpu.SemaphoreType.DMA((6,)),
            pltpu.SemaphoreType.DMA((2,)),
            pltpu.SemaphoreType.DMA((2,)),
            pltpu.SemaphoreType.DMA,
            pltpu.SemaphoreType.DMA,
        ],
        compiler_params=pltpu.CompilerParams(collective_id=0, has_side_effects=True),
        name="sums",
    )(state, face_nbr, halo_send, face_area, flux_left, flux_right)
    return pl.pallas_call(
        invert_kernel,
        out_shape=jax.ShapeDtypeStruct((2, NVAR, NVAR, HARM, share), f32),
        in_specs=[vmem, vmem, smem, smem],
        out_specs=vmem,
        name="invert",
    )(sums, cell_volume.reshape(1, share), flux_left, flux_right)


def solution(mesh):
    placed = (
        P("inst", None, "space"),
        P(None, "space"),
        P(None, "space"),
        P(None, None, "space"),
        P(("space", "inst")),
        P(),
        P(),
    )
    return jax.shard_map(
        per_device,
        mesh=mesh,
        in_specs=placed,
        out_specs=P(None, None, None, None, ("space", "inst")),
        check_vma=False,
    )
```

```python
import functools

import jax
import jax.numpy as jnp
from jax import lax
from jax.experimental import pallas as pl
from jax.experimental.pallas import tpu as pltpu
from jax.sharding import PartitionSpec as P

INSTANCES = 32
HARM = 16
NVAR = 7
FACES = 6
LANES = 128

frequency = 0.1


def lane_gather(rows, lane):
    return jnp.take_along_axis(rows, lane, axis=1, mode="promise_in_bounds")


def wide(row):
    return jnp.broadcast_to(row, (8, LANES))


def bits_select(rows, index, bits):
    for b in range(bits):
        odd = ((index >> b) & 1) == 1
        rows = [jnp.where(odd, rows[k + 1], rows[k]) for k in range(0, len(rows), 2)]
    return rows[0]


def three_parts(value):
    high, rest = two_parts(value)
    return high, rest, ((value - high) - rest).astype(jnp.bfloat16).astype(jnp.float32)


def two_parts(value):
    high = value.astype(jnp.bfloat16).astype(jnp.float32)
    return high, (value - high).astype(jnp.bfloat16).astype(jnp.float32)


def sums_kernel(
    slabs, owners,
    state_hbm, nbr_hbm, send_hbm, area_hbm, volume_hbm, left_hbm, right_hbm,
    out,
    state, nbr, send, area, volume, left, right,
    idx, areas, halo_idx, up, down, from_low, from_high, table_rows, table, factors, weights,
    near, work, outbox, inbox,
    in_sem, halo_send_sem, halo_recv_sem, send_sem, recv_sem,
):
    space = lax.axis_index("space")
    inst = lax.axis_index("inst")
    has_above = space < slabs - 1
    has_below = space > 0
    above = lax.rem(space + 1, slabs)
    below = lax.rem(space + slabs - 1, slabs)
    f32 = jnp.float32
    bf16 = jnp.bfloat16

    loads = [
        pltpu.make_async_copy(src, dst, in_sem.at[k])
        for k, (src, dst) in enumerate(
            [
                (left_hbm, left), (right_hbm, right), (send_hbm, send), (state_hbm, state),
                (nbr_hbm, nbr), (area_hbm, area), (volume_hbm, volume),
            ]
        )
    ]
    for load in loads:
        load.start()

    barrier = pltpu.get_barrier_semaphore()

    @pl.when(has_above)
    def _():
        pl.semaphore_signal(barrier, inc=1, device_id={"space": above}, device_id_type=pl.DeviceIdType.MESH)

    @pl.when(has_below)
    def _():
        pl.semaphore_signal(barrier, inc=1, device_id={"space": below}, device_id_type=pl.DeviceIdType.MESH)

    def greet(step, carry):
        other = lax.rem(inst + step, owners)
        pl.semaphore_signal(barrier, inc=1, device_id={"inst": other}, device_id_type=pl.DeviceIdType.MESH)
        return carry

    lax.fori_loop(1, owners, greet, 0)

    loads[2].wait()
    loads[3].wait()
    for k in range(4):
        halo_idx[pl.ds(k, 1)] = send[0:1, LANES * k : LANES * (k + 1)]
        halo_idx[pl.ds(4 + k, 1)] = send[1:2, LANES * k : LANES * (k + 1)]
    hidx = halo_idx[...]
    hlane = hidx & (LANES - 1)
    hrow = (hidx >> 7) & 3
    upper = lax.broadcasted_iota(jnp.int32, (8, LANES), 0) < 4
    for c in range(NVAR):
        found = jnp.zeros((8, LANES), f32)
        for q in range(4):
            rows = jnp.where(upper, wide(state[c, pl.ds(28 + q, 1)]), wide(state[c, pl.ds(q, 1)]))
            found = jnp.where(hrow == q, lane_gather(rows, hlane), found)
        up[pl.ds(4 * c, 4)] = found[0:4]
        down[pl.ds(4 * c, 4)] = found[4:8]

    pl.semaphore_wait(barrier, owners - 1 + has_above.astype(jnp.int32) + has_below.astype(jnp.int32))
    rise = pltpu.make_async_remote_copy(
        src_ref=up, dst_ref=from_low, send_sem=halo_send_sem.at[0], recv_sem=halo_recv_sem.at[0],
        device_id={"space": above}, device_id_type=pl.DeviceIdType.MESH,
    )
    sink = pltpu.make_async_remote_copy(
        src_ref=down, dst_ref=from_high, send_sem=halo_send_sem.at[1], recv_sem=halo_recv_sem.at[1],
        device_id={"space": below}, device_id_type=pl.DeviceIdType.MESH,
    )

    @pl.when(has_above)
    def _():
        rise.start()

    @pl.when(has_below)
    def _():
        sink.start()

    loads[0].wait()
    loads[1].wait()
    factors[...] = jnp.zeros_like(factors)
    factors[0:NVAR, 0:NVAR] = left[...]
    factors[8 : 8 + NVAR, 0:NVAR] = right[...]
    eye = (
        lax.broadcasted_iota(jnp.int32, (8, LANES), 0) == lax.broadcasted_iota(jnp.int32, (8, LANES), 1)
    ).astype(f32)
    turned = lax.dot_general(
        eye, jnp.concatenate([factors[8:16], jnp.zeros((120, LANES), f32)], axis=0),
        (((1,), (1,)), ((), ())), precision=lax.Precision.HIGHEST, preferred_element_type=f32,
    )
    lane_at = lax.broadcasted_iota(jnp.int32, (8, LANES), 1)
    row_at = lax.broadcasted_iota(jnp.int32, (8, LANES), 0)
    for j in range(NVAR):
        line = factors[0:8] * wide(turned[j : j + 1])
        line = jnp.where((lane_at == NVAR) & (row_at == j), 1.0, line)
        high, rest, last = three_parts(line)
        packed = high + pltpu.roll(high, 8, 1) + pltpu.roll(rest, 16, 1) + pltpu.roll(rest, 24, 1)
        packed = packed + pltpu.roll(high, 32, 1) + pltpu.roll(last, 40, 1)
        weights[8 * j : 8 * j + 8] = packed.astype(bf16)

    for c in range(NVAR):
        table_rows[pl.ds(c, 32, stride=8)] = state[c]
    table_rows[pl.ds(NVAR, 32, stride=8)] = jnp.zeros((32, LANES), f32)
    high, rest = two_parts(table_rows[...])
    table[:, 0:LANES] = high.astype(bf16)
    table[:, LANES : 2 * LANES] = rest.astype(bf16)

    loads[4].wait()

    def regroup(k, carry):
        q = k // 8
        s = lax.rem(k, 8)
        col = pl.multiple_of(k * LANES, LANES)
        idx[pl.ds(q * 48 + s, FACES, stride=8)] = nbr[:, pl.ds(col, LANES)]
        return carry

    lax.fori_loop(0, 32, regroup, 0, unroll=8)

    def by_lanes(g):
        cells = idx[pl.ds(pl.multiple_of(g * 8, 8), 8)]
        lane = cells & (LANES - 1)
        row = cells >> 7
        found = [jnp.zeros((8, LANES), f32) for _ in range(NVAR)]
        for r in range(32):
            here = row == r
            for c in range(NVAR):
                found[c] = jnp.where(here, lane_gather(wide(state[c, pl.ds(r, 1)]), lane), found[c])
        for c in range(NVAR):
            near[pl.ds(g * 64 + c, 8, stride=8)] = found[c]

    position = lax.broadcasted_iota(jnp.int32, (LANES, LANES), 0).astype(f32).astype(bf16)

    def by_matrix(g):
        lines = [idx[pl.ds(g * 8 + a, 1)] for a in range(8)]
        chosen = []
        for line in lines:
            lane = jnp.broadcast_to((line & (LANES - 1)).astype(f32).astype(bf16), (LANES, LANES))
            one = jnp.where(position == lane, bf16(1), bf16(0))
            chosen.append(jnp.concatenate([one, one], axis=0))
        picked = jnp.dot(table[...], jnp.concatenate(chosen, axis=1), preferred_element_type=f32)
        for a in range(8):
            rows = [picked[8 * r : 8 * r + 8, LANES * a : LANES * (a + 1)] for r in range(32)]
            near[pl.ds(pl.multiple_of((g * 8 + a) * 8, 8), 8)] = bits_select(rows, wide(lines[a] >> 7), 5)

    loads[5].wait()

    def local(q, carry):
        for k in range(8):
            col = pl.multiple_of((q * 8 + k) * LANES, LANES)
            for x in range(3):
                areas[x, pl.ds(q * 48 + k, FACES, stride=8)] = area[x, :, pl.ds(col, LANES)]
        for d in range(FACES):
            if d < 2:
                by_lanes(q * FACES + d)
            else:
                by_matrix(q * FACES + d)
        return carry

    lax.fori_loop(0, 4, local, 0)

    @pl.when(has_below)
    def _():
        rise.wait_recv()

    @pl.when(has_above)
    def _():
        sink.wait_recv()

    @pl.when(space == 0)
    def _():
        from_low[...] = jnp.zeros_like(from_low)

    @pl.when(space == slabs - 1)
    def _():
        from_high[...] = jnp.zeros_like(from_high)

    def group(q, carry):
        first = pl.multiple_of(q * 8, 8)
        totals = [jnp.zeros((8, LANES), f32) for _ in range(8)]
        for d in range(FACES):
            g = q * FACES + d
            at = pl.multiple_of(g * 8, 8)
            cells = idx[pl.ds(at, 8)]
            lane = cells & (LANES - 1)
            row = cells >> 7
            found = [near[pl.ds(g * 64 + c, 8, stride=8)] for c in range(NVAR)]
            for r in range(8):
                here = row == 32 + r
                source = from_low if r < 4 else from_high
                for c in range(NVAR):
                    line = source[pl.ds(4 * c + r % 4, 1)]
                    found[c] = jnp.where(here, lane_gather(wide(line), lane), found[c])
            mean = [0.5 * (state[c, pl.ds(first, 8)] + found[c]) for c in range(NVAR)]
            flux = (
                mean[1] * areas[0, pl.ds(at, 8)]
                + mean[2] * areas[1, pl.ds(at, 8)]
                + mean[3] * areas[2, pl.ds(at, 8)]
            )
            for c in range(8):
                work[d, pl.ds(c, 8, stride=8)] = mean[c] if c < NVAR else flux
            columns = []
            for a in range(8):
                high, rest = two_parts(work[d, 8 * a : 8 * a + 8])
                columns.append(jnp.concatenate([high, rest, high, rest], axis=0).astype(bf16))
            entries = jnp.dot(weights[:, 0:32], jnp.concatenate(columns, axis=1), preferred_element_type=f32)
            for a in range(8):
                row_sum = None
                for j in range(NVAR):
                    entry = jnp.abs(entries[8 * j : 8 * j + 8, LANES * a : LANES * (a + 1)])
                    row_sum = entry if row_sum is None else row_sum + entry
                work[d, 8 * a : 8 * a + 8] = row_sum
            largest = work[d, pl.ds(0, 8, stride=8)]
            for i in range(1, NVAR):
                largest = jnp.maximum(largest, work[d, pl.ds(i, 8, stride=8)])
            last = flux + (largest + 0.5)
            totals = [t + x for t, x in zip(totals, mean + [last])]
        for c in range(8):
            outbox[pl.ds(q * 64 + c, 8, stride=8)] = totals[c]

        def post(k, carry):
            owner = q * 8 + k

            @pl.when(owner != inst)
            def _():
                slot = lax.rem(inst - owner + owners, owners) - 1
                pltpu.make_async_remote_copy(
                    src_ref=outbox.at[pl.ds(pl.multiple_of(owner * 8, 8), 8)],
                    dst_ref=inbox.at[pl.ds(pl.multiple_of(slot * 8, 8), 8)],
                    send_sem=send_sem, recv_sem=recv_sem,
                    device_id={"inst": owner}, device_id_type=pl.DeviceIdType.MESH,
                ).start()

            return carry

        lax.fori_loop(0, 8, post, 0)
        return carry

    lax.fori_loop(0, 4, group, 0)
    pltpu.make_async_copy(inbox, inbox, recv_sem).wait()
    total = outbox[pl.ds(pl.multiple_of(inst * 8, 8), 8)]
    for k in range(31):
        total = total + inbox[8 * k : 8 * k + 8]
    high, rest, last = three_parts(total)
    parts = jnp.concatenate([high, rest, high, rest, last, high], axis=0).astype(bf16)
    out[0:56] = jnp.dot(weights[:, 0:48], parts, preferred_element_type=f32) * (0.5 / (FACES * INSTANCES))
    loads[6].wait()
    out[56:64] = frequency * wide(volume[...])
    pltpu.make_async_copy(inbox, inbox, send_sem).wait()

    @pl.when(has_above)
    def _():
        rise.wait_send()

    @pl.when(has_below)
    def _():
        sink.wait_send()


def invert_kernel(mean, out):
    harmonic = lax.broadcasted_iota(jnp.int32, (HARM, LANES), 0).astype(jnp.float32) + 1.0
    shift = harmonic * jnp.broadcast_to(mean[pl.ds(56, 1)], (HARM, LANES))
    real = {}
    imag = {}
    for i in range(NVAR):
        for j in range(NVAR):
            real[i, j] = jnp.broadcast_to(mean[pl.ds(8 * j + i, 1)], (HARM, LANES))
            imag[i, j] = shift if i == j else None

    def product(ar, ai, br, bi):
        if ai is None and bi is None:
            return ar * br, None
        if ai is None:
            return ar * br, ar * bi
        if bi is None:
            return ar * br, ai * br
        return ar * br - ai * bi, ar * bi + ai * br

    for k in range(NVAR):
        pr, pi = real[k, k], imag[k, k]
        norm = 1.0 / (pr * pr + pi * pi)
        pr, pi = pr * norm, -pi * norm
        for j in range(NVAR):
            if j != k:
                real[k, j], imag[k, j] = product(real[k, j], imag[k, j], pr, pi)
        real[k, k], imag[k, k] = pr, pi
        for i in range(NVAR):
            if i == k:
                continue
            fr, fi = real[i, k], imag[i, k]
            for j in range(NVAR):
                if j == k:
                    continue
                xr, xi = product(fr, fi, real[k, j], imag[k, j])
                real[i, j] = real[i, j] - xr
                if xi is not None:
                    imag[i, j] = -xi if imag[i, j] is None else imag[i, j] - xi
            xr, xi = product(fr, fi, pr, pi)
            real[i, k], imag[i, k] = -xr, -xi
    for i in range(NVAR):
        for j in range(NVAR):
            out[0, i, j] = real[i, j]
            out[1, i, j] = imag[i, j]


def per_device(flow_state, face_nbr, halo_send, face_area, cell_volume, flux_left, flux_right):
    slabs = lax.axis_size("space")
    owners = lax.axis_size("inst")
    share = cell_volume.shape[0]
    state = flow_state.reshape(NVAR, 32, LANES)
    vmem = pl.BlockSpec(memory_space=pltpu.VMEM)
    f32 = jnp.float32
    mean = pl.pallas_call(
        functools.partial(sums_kernel, slabs, owners),
        out_shape=jax.ShapeDtypeStruct((64, LANES), f32),
        in_specs=[pl.BlockSpec(memory_space=pltpu.HBM)] * 7,
        out_specs=vmem,
        scratch_shapes=[
            pltpu.VMEM((NVAR, 32, LANES), f32),
            pltpu.VMEM(face_nbr.shape, jnp.int32),
            pltpu.VMEM(halo_send.shape, jnp.int32),
            pltpu.VMEM(face_area.shape, f32),
            pltpu.VMEM((1, share), f32),
            pltpu.VMEM((NVAR, NVAR), f32),
            pltpu.VMEM((NVAR, NVAR), f32),
            pltpu.VMEM((192, LANES), jnp.int32),
            pltpu.VMEM((3, 192, LANES), f32),
            pltpu.VMEM((8, LANES), jnp.int32),
            pltpu.VMEM((28, LANES), f32),
            pltpu.VMEM((28, LANES), f32),
            pltpu.VMEM((28, LANES), f32),
            pltpu.VMEM((28, LANES), f32),
            pltpu.VMEM((256, LANES), f32),
            pltpu.VMEM((256, 2 * LANES), jnp.bfloat16),
            pltpu.VMEM((16, LANES), f32),
            pltpu.VMEM((56, LANES), jnp.bfloat16),
            pltpu.VMEM((1536, LANES), f32),
            pltpu.VMEM((FACES, 64, LANES), f32),
            pltpu.VMEM((256, LANES), f32),
            pltpu.VMEM((248, LANES), f32),
            pltpu.SemaphoreType.DMA((7,)),
            pltpu.SemaphoreType.DMA((2,)),
            pltpu.SemaphoreType.DMA((2,)),
            pltpu.SemaphoreType.DMA,
            pltpu.SemaphoreType.DMA,
        ],
        compiler_params=pltpu.CompilerParams(collective_id=0, has_side_effects=True),
        name="sums",
    )(state, face_nbr, halo_send, face_area, cell_volume.reshape(1, share), flux_left, flux_right)
    return pl.pallas_call(
        invert_kernel,
        out_shape=jax.ShapeDtypeStruct((2, NVAR, NVAR, HARM, share), f32),
        in_specs=[vmem],
        out_specs=vmem,
        name="invert",
    )(mean)


def solution(mesh):
    placed = (
        P("inst", None, "space"),
        P(None, "space"),
        P(None, "space"),
        P(None, None, "space"),
        P(("space", "inst")),
        P(),
        P(),
    )
    return jax.shard_map(
        per_device,
        mesh=mesh,
        in_specs=placed,
        out_specs=P(None, None, None, None, ("space", "inst")),
        check_vma=False,
    )
```

```python
import functools

import jax
import jax.numpy as jnp
from jax import lax
from jax.experimental import pallas as pl
from jax.experimental.pallas import tpu as pltpu
from jax.sharding import PartitionSpec as P

INSTANCES = 32
HARM = 16
NVAR = 7
FACES = 6
LANES = 128

frequency = 0.1


def lane_gather(rows, lane):
    return jnp.take_along_axis(rows, lane, axis=1, mode="promise_in_bounds")


def wide(row):
    return jnp.broadcast_to(row, (8, LANES))


def bits_select(rows, index, bits):
    for b in range(bits):
        odd = ((index >> b) & 1) == 1
        rows = [jnp.where(odd, rows[k + 1], rows[k]) for k in range(0, len(rows), 2)]
    return rows[0]


def three_parts(value):
    high, rest = two_parts(value)
    return high, rest, ((value - high) - rest).astype(jnp.bfloat16).astype(jnp.float32)


def two_parts(value):
    high = value.astype(jnp.bfloat16).astype(jnp.float32)
    return high, (value - high).astype(jnp.bfloat16).astype(jnp.float32)


def sums_kernel(
    slabs, owners,
    state_hbm, nbr_hbm, send_hbm, area_hbm, volume_hbm, left_hbm, right_hbm,
    out,
    state, nbr, send, area, volume, left, right,
    idx, areas, halo_idx, up, down, from_low, from_high, table_rows, table, factors, weights,
    near, work, outbox, inbox,
    in_sem, halo_send_sem, halo_recv_sem, send_sem, recv_sem,
):
    space = lax.axis_index("space")
    inst = lax.axis_index("inst")
    has_above = space < slabs - 1
    has_below = space > 0
    above = lax.rem(space + 1, slabs)
    below = lax.rem(space + slabs - 1, slabs)
    f32 = jnp.float32
    bf16 = jnp.bfloat16

    loads = [
        pltpu.make_async_copy(src, dst, in_sem.at[k])
        for k, (src, dst) in enumerate(
            [
                (left_hbm, left), (right_hbm, right), (send_hbm, send), (state_hbm, state),
                (nbr_hbm, nbr), (area_hbm, area), (volume_hbm, volume),
            ]
        )
    ]
    for load in loads:
        load.start()

    barrier = pltpu.get_barrier_semaphore()

    @pl.when(has_above)
    def _():
        pl.semaphore_signal(barrier, inc=1, device_id={"space": above}, device_id_type=pl.DeviceIdType.MESH)

    @pl.when(has_below)
    def _():
        pl.semaphore_signal(barrier, inc=1, device_id={"space": below}, device_id_type=pl.DeviceIdType.MESH)

    for step in [*range(23, 15, -1), *range(31, 23, -1), *range(15, 0, -1)]:
        pl.semaphore_signal(barrier, inc=1, device_id={"inst": inst ^ step}, device_id_type=pl.DeviceIdType.MESH)

    loads[2].wait()
    loads[3].wait()
    for k in range(4):
        halo_idx[pl.ds(k, 1)] = send[0:1, LANES * k : LANES * (k + 1)]
        halo_idx[pl.ds(4 + k, 1)] = send[1:2, LANES * k : LANES * (k + 1)]
    hidx = halo_idx[...]
    hlane = hidx & (LANES - 1)
    hrow = (hidx >> 7) & 3
    upper = lax.broadcasted_iota(jnp.int32, (8, LANES), 0) < 4
    for c in range(NVAR):
        found = jnp.zeros((8, LANES), f32)
        for q in range(4):
            rows = jnp.where(upper, wide(state[c, pl.ds(28 + q, 1)]), wide(state[c, pl.ds(q, 1)]))
            found = jnp.where(hrow == q, lane_gather(rows, hlane), found)
        up[pl.ds(4 * c, 4)] = found[0:4]
        down[pl.ds(4 * c, 4)] = found[4:8]

    pl.semaphore_wait(barrier, owners - 1 + has_above.astype(jnp.int32) + has_below.astype(jnp.int32))
    rise = pltpu.make_async_remote_copy(
        src_ref=up, dst_ref=from_low, send_sem=halo_send_sem.at[0], recv_sem=halo_recv_sem.at[0],
        device_id={"space": above}, device_id_type=pl.DeviceIdType.MESH,
    )
    sink = pltpu.make_async_remote_copy(
        src_ref=down, dst_ref=from_high, send_sem=halo_send_sem.at[1], recv_sem=halo_recv_sem.at[1],
        device_id={"space": below}, device_id_type=pl.DeviceIdType.MESH,
    )

    @pl.when(has_above)
    def _():
        rise.start()

    @pl.when(has_below)
    def _():
        sink.start()

    loads[0].wait()
    loads[1].wait()
    factors[...] = jnp.zeros_like(factors)
    factors[0:NVAR, 0:NVAR] = left[...]
    factors[8 : 8 + NVAR, 0:NVAR] = right[...]
    eye = (
        lax.broadcasted_iota(jnp.int32, (8, LANES), 0) == lax.broadcasted_iota(jnp.int32, (8, LANES), 1)
    ).astype(f32)
    turned = lax.dot_general(
        eye, jnp.concatenate([factors[8:16], jnp.zeros((120, LANES), f32)], axis=0),
        (((1,), (1,)), ((), ())), precision=lax.Precision.HIGHEST, preferred_element_type=f32,
    )
    lane_at = lax.broadcasted_iota(jnp.int32, (8, LANES), 1)
    row_at = lax.broadcasted_iota(jnp.int32, (8, LANES), 0)
    for j in range(NVAR):
        line = factors[0:8] * wide(turned[j : j + 1])
        line = jnp.where((lane_at == NVAR) & (row_at == j), 1.0, line)
        high, rest, last = three_parts(line)
        packed = high + pltpu.roll(high, 8, 1) + pltpu.roll(rest, 16, 1) + pltpu.roll(rest, 24, 1)
        packed = packed + pltpu.roll(high, 32, 1) + pltpu.roll(last, 40, 1)
        weights[8 * j : 8 * j + 8] = packed.astype(bf16)

    for c in range(NVAR):
        table_rows[pl.ds(c, 32, stride=8)] = state[c]
    table_rows[pl.ds(NVAR, 32, stride=8)] = jnp.zeros((32, LANES), f32)
    high, rest = two_parts(table_rows[...])
    table[:, 0:LANES] = high.astype(bf16)
    table[:, LANES : 2 * LANES] = rest.astype(bf16)

    loads[4].wait()

    def regroup(k, carry):
        q = k // 8
        s = lax.rem(k, 8)
        col = pl.multiple_of(k * LANES, LANES)
        idx[pl.ds(q * 48 + s, FACES, stride=8)] = nbr[:, pl.ds(col, LANES)]
        return carry

    lax.fori_loop(0, 32, regroup, 0, unroll=8)

    def by_lanes(g):
        cells = idx[pl.ds(pl.multiple_of(g * 8, 8), 8)]
        lane = cells & (LANES - 1)
        row = cells >> 7
        found = [jnp.zeros((8, LANES), f32) for _ in range(NVAR)]
        for r in range(32):
            here = row == r
            for c in range(NVAR):
                found[c] = jnp.where(here, lane_gather(wide(state[c, pl.ds(r, 1)]), lane), found[c])
        for c in range(NVAR):
            near[pl.ds(g * 64 + c, 8, stride=8)] = found[c]

    position = lax.broadcasted_iota(jnp.int32, (LANES, LANES), 0).astype(f32).astype(bf16)

    def by_matrix(g):
        lines = [idx[pl.ds(g * 8 + a, 1)] for a in range(8)]
        chosen = []
        for line in lines:
            lane = jnp.broadcast_to((line & (LANES - 1)).astype(f32).astype(bf16), (LANES, LANES))
            one = jnp.where(position == lane, bf16(1), bf16(0))
            chosen.append(jnp.concatenate([one, one], axis=0))
        picked = jnp.dot(table[...], jnp.concatenate(chosen, axis=1), preferred_element_type=f32)
        for a in range(8):
            rows = [picked[8 * r : 8 * r + 8, LANES * a : LANES * (a + 1)] for r in range(32)]
            near[pl.ds(pl.multiple_of((g * 8 + a) * 8, 8), 8)] = bits_select(rows, wide(lines[a] >> 7), 5)

    loads[5].wait()

    def local(q, carry):
        for k in range(8):
            col = pl.multiple_of((q * 8 + k) * LANES, LANES)
            for x in range(3):
                areas[x, pl.ds(q * 48 + k, FACES, stride=8)] = area[x, :, pl.ds(col, LANES)]
        for d in range(FACES):
            if d < 2:
                by_lanes(q * FACES + d)
            else:
                by_matrix(q * FACES + d)
        return carry

    lax.fori_loop(0, 4, local, 0)

    @pl.when(has_below)
    def _():
        rise.wait_recv()

    @pl.when(has_above)
    def _():
        sink.wait_recv()

    @pl.when(space == 0)
    def _():
        from_low[...] = jnp.zeros_like(from_low)

    @pl.when(space == slabs - 1)
    def _():
        from_high[...] = jnp.zeros_like(from_high)

    def group(q, own):
        first = pl.multiple_of(q * 8, 8)
        totals = [jnp.zeros((8, LANES), f32) for _ in range(8)]
        for d in range(FACES):
            g = q * FACES + d
            at = pl.multiple_of(g * 8, 8)
            cells = idx[pl.ds(at, 8)]
            lane = cells & (LANES - 1)
            row = cells >> 7
            found = [near[pl.ds(g * 64 + c, 8, stride=8)] for c in range(NVAR)]
            for r in range(8):
                here = row == 32 + r
                source = from_low if r < 4 else from_high
                for c in range(NVAR):
                    line = source[pl.ds(4 * c + r % 4, 1)]
                    found[c] = jnp.where(here, lane_gather(wide(line), lane), found[c])
            mean = [0.5 * (state[c, pl.ds(first, 8)] + found[c]) for c in range(NVAR)]
            flux = (
                mean[1] * areas[0, pl.ds(at, 8)]
                + mean[2] * areas[1, pl.ds(at, 8)]
                + mean[3] * areas[2, pl.ds(at, 8)]
            )
            for c in range(8):
                work[d, pl.ds(c, 8, stride=8)] = mean[c] if c < NVAR else flux
            columns = []
            for a in range(8):
                high, rest = two_parts(work[d, 8 * a : 8 * a + 8])
                columns.append(jnp.concatenate([high, rest, high, rest], axis=0).astype(bf16))
            entries = jnp.dot(weights[:, 0:32], jnp.concatenate(columns, axis=1), preferred_element_type=f32)
            for a in range(8):
                row_sum = None
                for j in range(NVAR):
                    entry = jnp.abs(entries[8 * j : 8 * j + 8, LANES * a : LANES * (a + 1)])
                    row_sum = entry if row_sum is None else row_sum + entry
                work[d, 8 * a : 8 * a + 8] = row_sum
            largest = work[d, pl.ds(0, 8, stride=8)]
            for i in range(1, NVAR):
                largest = jnp.maximum(largest, work[d, pl.ds(i, 8, stride=8)])
            last = flux + (largest + 0.5)
            totals = [t + x for t, x in zip(totals, mean + [last])]
        for c in range(8):
            outbox[pl.ds(q * 64 + c, 8, stride=8)] = totals[c]

        for r in range(7, 0 if own else -1, -1):
            owner = q * 8 + (low ^ r)
            slot = lax.rem(inst - owner + owners, owners) - 1
            pltpu.make_async_remote_copy(
                src_ref=outbox.at[pl.ds(pl.multiple_of(owner * 8, 8), 8)],
                dst_ref=inbox.at[pl.ds(pl.multiple_of(slot * 8, 8), 8)],
                send_sem=send_sem, recv_sem=recv_sem,
                device_id={"inst": owner}, device_id_type=pl.DeviceIdType.MESH,
            ).start()

    mine = inst // 8
    low = lax.rem(inst, 8)
    for away in (2, 1, 3):
        group(lax.rem(mine + away, 4), False)
    group(mine, True)
    pltpu.make_async_copy(inbox, inbox, recv_sem).wait()
    total = outbox[pl.ds(pl.multiple_of(inst * 8, 8), 8)]
    for k in range(31):
        total = total + inbox[8 * k : 8 * k + 8]
    high, rest, last = three_parts(total)
    parts = jnp.concatenate([high, rest, high, rest, last, high], axis=0).astype(bf16)
    out[0:56] = jnp.dot(weights[:, 0:48], parts, preferred_element_type=f32) * (0.5 / (FACES * INSTANCES))
    loads[6].wait()
    out[56:64] = frequency * wide(volume[...])
    pltpu.make_async_copy(inbox, inbox, send_sem).wait()

    @pl.when(has_above)
    def _():
        rise.wait_send()

    @pl.when(has_below)
    def _():
        sink.wait_send()


def invert_kernel(mean, out):
    harmonic = lax.broadcasted_iota(jnp.int32, (HARM, LANES), 0).astype(jnp.float32) + 1.0
    shift = harmonic * jnp.broadcast_to(mean[pl.ds(56, 1)], (HARM, LANES))
    real = {}
    imag = {}
    for i in range(NVAR):
        for j in range(NVAR):
            real[i, j] = jnp.broadcast_to(mean[pl.ds(8 * j + i, 1)], (HARM, LANES))
            imag[i, j] = shift if i == j else None

    def product(ar, ai, br, bi):
        if ai is None and bi is None:
            return ar * br, None
        if ai is None:
            return ar * br, ar * bi
        if bi is None:
            return ar * br, ai * br
        return ar * br - ai * bi, ar * bi + ai * br

    for k in range(NVAR):
        pr, pi = real[k, k], imag[k, k]
        norm = 1.0 / (pr * pr + pi * pi)
        pr, pi = pr * norm, -pi * norm
        for j in range(NVAR):
            if j != k:
                real[k, j], imag[k, j] = product(real[k, j], imag[k, j], pr, pi)
        real[k, k], imag[k, k] = pr, pi
        for i in range(NVAR):
            if i == k:
                continue
            fr, fi = real[i, k], imag[i, k]
            for j in range(NVAR):
                if j == k:
                    continue
                xr, xi = product(fr, fi, real[k, j], imag[k, j])
                real[i, j] = real[i, j] - xr
                if xi is not None:
                    imag[i, j] = -xi if imag[i, j] is None else imag[i, j] - xi
            xr, xi = product(fr, fi, pr, pi)
            real[i, k], imag[i, k] = -xr, -xi
    for i in range(NVAR):
        for j in range(NVAR):
            out[0, i, j] = real[i, j]
            out[1, i, j] = imag[i, j]


def per_device(flow_state, face_nbr, halo_send, face_area, cell_volume, flux_left, flux_right):
    slabs = lax.axis_size("space")
    owners = lax.axis_size("inst")
    share = cell_volume.shape[0]
    state = flow_state.reshape(NVAR, 32, LANES)
    vmem = pl.BlockSpec(memory_space=pltpu.VMEM)
    f32 = jnp.float32
    mean = pl.pallas_call(
        functools.partial(sums_kernel, slabs, owners),
        out_shape=jax.ShapeDtypeStruct((64, LANES), f32),
        in_specs=[pl.BlockSpec(memory_space=pltpu.HBM)] * 7,
        out_specs=vmem,
        scratch_shapes=[
            pltpu.VMEM((NVAR, 32, LANES), f32),
            pltpu.VMEM(face_nbr.shape, jnp.int32),
            pltpu.VMEM(halo_send.shape, jnp.int32),
            pltpu.VMEM(face_area.shape, f32),
            pltpu.VMEM((1, share), f32),
            pltpu.VMEM((NVAR, NVAR), f32),
            pltpu.VMEM((NVAR, NVAR), f32),
            pltpu.VMEM((192, LANES), jnp.int32),
            pltpu.VMEM((3, 192, LANES), f32),
            pltpu.VMEM((8, LANES), jnp.int32),
            pltpu.VMEM((28, LANES), f32),
            pltpu.VMEM((28, LANES), f32),
            pltpu.VMEM((28, LANES), f32),
            pltpu.VMEM((28, LANES), f32),
            pltpu.VMEM((256, LANES), f32),
            pltpu.VMEM((256, 2 * LANES), jnp.bfloat16),
            pltpu.VMEM((16, LANES), f32),
            pltpu.VMEM((56, LANES), jnp.bfloat16),
            pltpu.VMEM((1536, LANES), f32),
            pltpu.VMEM((FACES, 64, LANES), f32),
            pltpu.VMEM((256, LANES), f32),
            pltpu.VMEM((248, LANES), f32),
            pltpu.SemaphoreType.DMA((7,)),
            pltpu.SemaphoreType.DMA((2,)),
            pltpu.SemaphoreType.DMA((2,)),
            pltpu.SemaphoreType.DMA,
            pltpu.SemaphoreType.DMA,
        ],
        compiler_params=pltpu.CompilerParams(collective_id=0, has_side_effects=True, vmem_limit_bytes=24 << 20),
        name="sums",
    )(*[
        pltpu.with_memory_space_constraint(x, pltpu.HBM)
        for x in (state, face_nbr, halo_send, face_area, cell_volume.reshape(1, share), flux_left, flux_right)
    ])
    return pl.pallas_call(
        invert_kernel,
        out_shape=jax.ShapeDtypeStruct((2, NVAR, NVAR, HARM, share), f32),
        in_specs=[vmem],
        out_specs=vmem,
        compiler_params=pltpu.CompilerParams(vmem_limit_bytes=8 << 20),
        name="invert",
    )(mean)


def solution(mesh):
    placed = (
        P("inst", None, "space"),
        P(None, "space"),
        P(None, "space"),
        P(None, None, "space"),
        P(("space", "inst")),
        P(),
        P(),
    )
    return jax.shard_map(
        per_device,
        mesh=mesh,
        in_specs=placed,
        out_specs=P(None, None, None, None, ("space", "inst")),
        check_vma=False,
    )
```

```python
import functools

import jax
import jax.numpy as jnp
from jax import lax
from jax.experimental import pallas as pl
from jax.experimental.pallas import tpu as pltpu
from jax.sharding import PartitionSpec as P

INSTANCES = 32
HARM = 16
NVAR = 7
FACES = 6
LANES = 128

frequency = 0.1


def lane_gather(rows, lane):
    return jnp.take_along_axis(rows, lane, axis=1, mode="promise_in_bounds")


def wide(row):
    return jnp.broadcast_to(row, (8, LANES))


def bits_select(rows, index, bits):
    for b in range(bits):
        odd = ((index >> b) & 1) == 1
        rows = [jnp.where(odd, rows[k + 1], rows[k]) for k in range(0, len(rows), 2)]
    return rows[0]


def three_parts(value):
    high, rest = two_parts(value)
    return high, rest, ((value - high) - rest).astype(jnp.bfloat16).astype(jnp.float32)


def two_parts(value):
    high = value.astype(jnp.bfloat16).astype(jnp.float32)
    return high, (value - high).astype(jnp.bfloat16).astype(jnp.float32)


def sums_kernel(
    slabs, owners,
    state_hbm, nbr_hbm, send_hbm, area_hbm, volume_hbm, left_hbm, right_hbm,
    out,
    state, nbr, send, area, volume, left, right,
    idx, areas, halo_idx, up, down, from_low, from_high, table_rows, table, factors, weights,
    near, work, outbox, inbox,
    in_sem, halo_send_sem, halo_recv_sem, send_sem, recv_sem, round_sem,
):
    space = lax.axis_index("space")
    inst = lax.axis_index("inst")
    has_above = space < slabs - 1
    has_below = space > 0
    above = lax.rem(space + 1, slabs)
    below = lax.rem(space + slabs - 1, slabs)
    f32 = jnp.float32
    bf16 = jnp.bfloat16

    loads = [
        pltpu.make_async_copy(src, dst, in_sem.at[k])
        for k, (src, dst) in enumerate(
            [
                (send_hbm, send), (state_hbm, state), (left_hbm, left), (right_hbm, right),
                (nbr_hbm, nbr), (area_hbm, area), (volume_hbm, volume),
            ]
        )
    ]
    for load in loads:
        load.start()

    barrier = pltpu.get_barrier_semaphore()

    @pl.when(has_above)
    def _():
        pl.semaphore_signal(barrier, inc=1, device_id={"space": above}, device_id_type=pl.DeviceIdType.MESH)

    @pl.when(has_below)
    def _():
        pl.semaphore_signal(barrier, inc=1, device_id={"space": below}, device_id_type=pl.DeviceIdType.MESH)

    for partner in (16, 6, 7, 4, 5, 8, 24, 2, 3, 1):
        pl.semaphore_signal(barrier, inc=1, device_id={"inst": inst ^ partner}, device_id_type=pl.DeviceIdType.MESH)

    loads[0].wait()
    loads[1].wait()
    for k in range(4):
        halo_idx[pl.ds(k, 1)] = send[0:1, LANES * k : LANES * (k + 1)]
        halo_idx[pl.ds(4 + k, 1)] = send[1:2, LANES * k : LANES * (k + 1)]
    hidx = halo_idx[...]
    hlane = hidx & (LANES - 1)
    hrow = (hidx >> 7) & 3
    upper = lax.broadcasted_iota(jnp.int32, (8, LANES), 0) < 4
    for c in range(NVAR):
        found = jnp.zeros((8, LANES), f32)
        for q in range(4):
            rows = jnp.where(upper, wide(state[c, pl.ds(28 + q, 1)]), wide(state[c, pl.ds(q, 1)]))
            found = jnp.where(hrow == q, lane_gather(rows, hlane), found)
        up[pl.ds(4 * c, 4)] = found[0:4]
        down[pl.ds(4 * c, 4)] = found[4:8]

    def prepare():
        loads[5].wait()
        loads[2].wait()
        loads[3].wait()
        factors[...] = jnp.zeros_like(factors)
        factors[0:NVAR, 0:NVAR] = left[...]
        factors[8 : 8 + NVAR, 0:NVAR] = right[...]
        eye = (
            lax.broadcasted_iota(jnp.int32, (8, LANES), 0) == lax.broadcasted_iota(jnp.int32, (8, LANES), 1)
        ).astype(f32)
        turned = lax.dot_general(
            eye, jnp.concatenate([factors[8:16], jnp.zeros((120, LANES), f32)], axis=0),
            (((1,), (1,)), ((), ())), precision=lax.Precision.HIGHEST, preferred_element_type=f32,
        )
        lane_at = lax.broadcasted_iota(jnp.int32, (8, LANES), 1)
        row_at = lax.broadcasted_iota(jnp.int32, (8, LANES), 0)
        for j in range(NVAR):
            line = factors[0:8] * wide(turned[j : j + 1])
            line = jnp.where((lane_at == NVAR) & (row_at == j), 1.0, line)
            high, rest, last = three_parts(line)
            packed = high + pltpu.roll(high, 8, 1) + pltpu.roll(rest, 16, 1) + pltpu.roll(rest, 24, 1)
            packed = packed + pltpu.roll(high, 32, 1) + pltpu.roll(last, 40, 1)
            weights[8 * j : 8 * j + 8] = packed.astype(bf16)

        for c in range(NVAR):
            table_rows[pl.ds(c, 32, stride=8)] = state[c]
        table_rows[pl.ds(NVAR, 32, stride=8)] = jnp.zeros((32, LANES), f32)
        high, rest = two_parts(table_rows[...])
        table[:, 0:LANES] = high.astype(bf16)
        table[:, LANES : 2 * LANES] = rest.astype(bf16)

        loads[4].wait()

        def regroup(k, carry):
            q = k // 8
            s = lax.rem(k, 8)
            col = pl.multiple_of(k * LANES, LANES)
            idx[pl.ds(q * 48 + s, FACES, stride=8)] = nbr[:, pl.ds(col, LANES)]
            return carry

        lax.fori_loop(0, 32, regroup, 0, unroll=8)

    def by_lanes(g):
        cells = idx[pl.ds(pl.multiple_of(g * 8, 8), 8)]
        lane = cells & (LANES - 1)
        row = cells >> 7
        found = [jnp.zeros((8, LANES), f32) for _ in range(NVAR)]
        for r in range(32):
            here = row == r
            for c in range(NVAR):
                found[c] = jnp.where(here, lane_gather(wide(state[c, pl.ds(r, 1)]), lane), found[c])
        for c in range(NVAR):
            near[pl.ds(g * 64 + c, 8, stride=8)] = found[c]

    position = lax.broadcasted_iota(jnp.int32, (LANES, LANES), 0).astype(f32).astype(bf16)

    def by_matrix(g):
        lines = [idx[pl.ds(g * 8 + a, 1)] for a in range(8)]
        chosen = []
        for line in lines:
            lane = jnp.broadcast_to((line & (LANES - 1)).astype(f32).astype(bf16), (LANES, LANES))
            one = jnp.where(position == lane, bf16(1), bf16(0))
            chosen.append(jnp.concatenate([one, one], axis=0))
        picked = jnp.dot(table[...], jnp.concatenate(chosen, axis=1), preferred_element_type=f32)
        for a in range(8):
            rows = [picked[8 * r : 8 * r + 8, LANES * a : LANES * (a + 1)] for r in range(32)]
            near[pl.ds(pl.multiple_of((g * 8 + a) * 8, 8), 8)] = bits_select(rows, wide(lines[a] >> 7), 5)

    def local(h, carry):
        for k in range(16):
            q = h * 2 + k // 8
            col = pl.multiple_of((h * 16 + k) * LANES, LANES)
            for x in range(3):
                areas[x, pl.ds(q * 48 + k % 8, FACES, stride=8)] = area[x, :, pl.ds(col, LANES)]
        for d in range(2 * FACES):
            if d in (0, 2, 5, 7, 10):
                by_lanes(h * 2 * FACES + d)
            else:
                by_matrix(h * 2 * FACES + d)
        return carry

    pl.semaphore_wait(barrier, 10 + has_above.astype(jnp.int32) + has_below.astype(jnp.int32))
    rise = pltpu.make_async_remote_copy(
        src_ref=up, dst_ref=from_low, send_sem=halo_send_sem.at[0], recv_sem=halo_recv_sem.at[0],
        device_id={"space": above}, device_id_type=pl.DeviceIdType.MESH,
    )
    sink = pltpu.make_async_remote_copy(
        src_ref=down, dst_ref=from_high, send_sem=halo_send_sem.at[1], recv_sem=halo_recv_sem.at[1],
        device_id={"space": below}, device_id_type=pl.DeviceIdType.MESH,
    )

    @pl.when(has_above)
    def _():
        rise.start()

    @pl.when(has_below)
    def _():
        sink.start()

    for partner in (16, 8, 24):
        pl.semaphore_signal(round_sem, inc=1, device_id={"inst": inst ^ partner}, device_id_type=pl.DeviceIdType.MESH)

    prepare()
    lax.fori_loop(0, 2, local, 0)


    @pl.when(has_below)
    def _():
        rise.wait_recv()

    @pl.when(has_above)
    def _():
        sink.wait_recv()

    @pl.when(space == 0)
    def _():
        from_low[...] = jnp.zeros_like(from_low)

    @pl.when(space == slabs - 1)
    def _():
        from_high[...] = jnp.zeros_like(from_high)

    def group(q, opening, own):
        first = pl.multiple_of(q * 8, 8)
        totals = [jnp.zeros((8, LANES), f32) for _ in range(8)]
        for d in range(FACES):
            g = q * FACES + d
            at = pl.multiple_of(g * 8, 8)
            cells = idx[pl.ds(at, 8)]
            lane = cells & (LANES - 1)
            row = cells >> 7
            found = [near[pl.ds(g * 64 + c, 8, stride=8)] for c in range(NVAR)]
            for r in range(8):
                here = row == 32 + r
                source = from_low if r < 4 else from_high
                for c in range(NVAR):
                    line = source[pl.ds(4 * c + r % 4, 1)]
                    found[c] = jnp.where(here, lane_gather(wide(line), lane), found[c])
            mean = [0.5 * (state[c, pl.ds(first, 8)] + found[c]) for c in range(NVAR)]
            flux = (
                mean[1] * areas[0, pl.ds(at, 8)]
                + mean[2] * areas[1, pl.ds(at, 8)]
                + mean[3] * areas[2, pl.ds(at, 8)]
            )
            for c in range(8):
                work[d, pl.ds(c, 8, stride=8)] = mean[c] if c < NVAR else flux
            columns = []
            for a in range(8):
                high, rest = two_parts(work[d, 8 * a : 8 * a + 8])
                columns.append(jnp.concatenate([high, rest, high, rest], axis=0).astype(bf16))
            entries = jnp.dot(weights[:, 0:32], jnp.concatenate(columns, axis=1), preferred_element_type=f32)
            for a in range(8):
                row_sum = None
                for j in range(NVAR):
                    entry = jnp.abs(entries[8 * j : 8 * j + 8, LANES * a : LANES * (a + 1)])
                    row_sum = entry if row_sum is None else row_sum + entry
                work[d, 8 * a : 8 * a + 8] = row_sum
            largest = work[d, pl.ds(0, 8, stride=8)]
            for i in range(1, NVAR):
                largest = jnp.maximum(largest, work[d, pl.ds(i, 8, stride=8)])
            last = flux + (largest + 0.5)
            totals = [t + x for t, x in zip(totals, mean + [last])]
        for c in range(8):
            outbox[pl.ds(q * 64 + c, 8, stride=8)] = totals[c]

        if opening:
            pl.semaphore_wait(round_sem, 3)
        for r in range(7, 0 if own else -1, -1):
            owner = q * 8 + (low ^ r)
            slot = lax.rem(inst - owner + owners, owners) - 1
            pltpu.make_async_remote_copy(
                src_ref=outbox.at[pl.ds(pl.multiple_of(owner * 8, 8), 8)],
                dst_ref=inbox.at[pl.ds(pl.multiple_of(slot * 8, 8), 8)],
                send_sem=send_sem, recv_sem=recv_sem,
                device_id={"inst": owner}, device_id_type=pl.DeviceIdType.MESH,
            ).start()

    mine = inst // 8
    low = lax.rem(inst, 8)
    for away in (2, 1, 3):
        group(lax.rem(mine + away, 4), away == 2, False)
    group(mine, False, True)
    pltpu.make_async_copy(inbox, inbox, recv_sem).wait()
    total = outbox[pl.ds(pl.multiple_of(inst * 8, 8), 8)]
    for k in range(31):
        total = total + inbox[8 * k : 8 * k + 8]
    high, rest, last = three_parts(total)
    parts = jnp.concatenate([high, rest, high, rest, last, high], axis=0).astype(bf16)
    out[0:56] = jnp.dot(weights[:, 0:48], parts, preferred_element_type=f32) * (0.5 / (FACES * INSTANCES))
    loads[6].wait()
    out[56:64] = frequency * wide(volume[...])
    pltpu.make_async_copy(inbox, inbox, send_sem).wait()

    @pl.when(has_above)
    def _():
        rise.wait_send()

    @pl.when(has_below)
    def _():
        sink.wait_send()


def invert_kernel(mean, out):
    harmonic = lax.broadcasted_iota(jnp.int32, (HARM, LANES), 0).astype(jnp.float32) + 1.0
    shift = harmonic * jnp.broadcast_to(mean[pl.ds(56, 1)], (HARM, LANES))
    real = {}
    imag = {}
    for i in range(NVAR):
        for j in range(NVAR):
            real[i, j] = jnp.broadcast_to(mean[pl.ds(8 * j + i, 1)], (HARM, LANES))
            imag[i, j] = shift if i == j else None

    def product(ar, ai, br, bi):
        if ai is None and bi is None:
            return ar * br, None
        if ai is None:
            return ar * br, ar * bi
        if bi is None:
            return ar * br, ai * br
        return ar * br - ai * bi, ar * bi + ai * br

    for k in range(NVAR):
        pr, pi = real[k, k], imag[k, k]
        norm = 1.0 / (pr * pr + pi * pi)
        pr, pi = pr * norm, -pi * norm
        for j in range(NVAR):
            if j != k:
                real[k, j], imag[k, j] = product(real[k, j], imag[k, j], pr, pi)
        real[k, k], imag[k, k] = pr, pi
        for i in range(NVAR):
            if i == k:
                continue
            fr, fi = real[i, k], imag[i, k]
            for j in range(NVAR):
                if j == k:
                    continue
                xr, xi = product(fr, fi, real[k, j], imag[k, j])
                real[i, j] = real[i, j] - xr
                if xi is not None:
                    imag[i, j] = -xi if imag[i, j] is None else imag[i, j] - xi
            xr, xi = product(fr, fi, pr, pi)
            real[i, k], imag[i, k] = -xr, -xi
    for i in range(NVAR):
        for j in range(NVAR):
            out[0, i, j] = real[i, j]
            out[1, i, j] = imag[i, j]


def per_device(flow_state, face_nbr, halo_send, face_area, cell_volume, flux_left, flux_right):
    slabs = lax.axis_size("space")
    owners = lax.axis_size("inst")
    share = cell_volume.shape[0]
    state = flow_state.reshape(NVAR, 32, LANES)
    vmem = pl.BlockSpec(memory_space=pltpu.VMEM)
    f32 = jnp.float32
    mean = pl.pallas_call(
        functools.partial(sums_kernel, slabs, owners),
        out_shape=jax.ShapeDtypeStruct((64, LANES), f32),
        in_specs=[pl.BlockSpec(memory_space=pltpu.HBM)] * 7,
        out_specs=vmem,
        scratch_shapes=[
            pltpu.VMEM((NVAR, 32, LANES), f32),
            pltpu.VMEM(face_nbr.shape, jnp.int32),
            pltpu.VMEM(halo_send.shape, jnp.int32),
            pltpu.VMEM(face_area.shape, f32),
            pltpu.VMEM((1, share), f32),
            pltpu.VMEM((NVAR, NVAR), f32),
            pltpu.VMEM((NVAR, NVAR), f32),
            pltpu.VMEM((192, LANES), jnp.int32),
            pltpu.VMEM((3, 192, LANES), f32),
            pltpu.VMEM((8, LANES), jnp.int32),
            pltpu.VMEM((28, LANES), f32),
            pltpu.VMEM((28, LANES), f32),
            pltpu.VMEM((28, LANES), f32),
            pltpu.VMEM((28, LANES), f32),
            pltpu.VMEM((256, LANES), f32),
            pltpu.VMEM((256, 2 * LANES), jnp.bfloat16),
            pltpu.VMEM((16, LANES), f32),
            pltpu.VMEM((56, LANES), jnp.bfloat16),
            pltpu.VMEM((1536, LANES), f32),
            pltpu.VMEM((FACES, 64, LANES), f32),
            pltpu.VMEM((256, LANES), f32),
            pltpu.VMEM((248, LANES), f32),
            pltpu.SemaphoreType.DMA((7,)),
            pltpu.SemaphoreType.DMA((2,)),
            pltpu.SemaphoreType.DMA((2,)),
            pltpu.SemaphoreType.DMA,
            pltpu.SemaphoreType.DMA,
            pltpu.SemaphoreType.REGULAR,
        ],
        compiler_params=pltpu.CompilerParams(collective_id=0, has_side_effects=True, vmem_limit_bytes=24 << 20),
        name="sums",
    )(*[
        pltpu.with_memory_space_constraint(x, pltpu.HBM)
        for x in (state, face_nbr, halo_send, face_area, cell_volume.reshape(1, share), flux_left, flux_right)
    ])
    return pl.pallas_call(
        invert_kernel,
        out_shape=jax.ShapeDtypeStruct((2, NVAR, NVAR, HARM, share), f32),
        in_specs=[vmem],
        out_specs=vmem,
        compiler_params=pltpu.CompilerParams(vmem_limit_bytes=8 << 20),
        name="invert",
    )(mean)


def solution(mesh):
    placed = (
        P("inst", None, "space"),
        P(None, "space"),
        P(None, "space"),
        P(None, None, "space"),
        P(("space", "inst")),
        P(),
        P(),
    )
    return jax.shard_map(
        per_device,
        mesh=mesh,
        in_specs=placed,
        out_specs=P(None, None, None, None, ("space", "inst")),
        check_vma=False,
    )
```

```python
import functools

import jax
import jax.numpy as jnp
from jax import lax
from jax.experimental import pallas as pl
from jax.experimental.pallas import tpu as pltpu
from jax.sharding import PartitionSpec as P

INSTANCES = 32
HARM = 16
NVAR = 7
FACES = 6
LANES = 128

frequency = 0.1


def lane_gather(rows, lane):
    return jnp.take_along_axis(rows, lane, axis=1, mode="promise_in_bounds")


def wide(row):
    return jnp.broadcast_to(row, (8, LANES))


def bits_select(rows, index, bits):
    for b in range(bits):
        odd = ((index >> b) & 1) == 1
        rows = [jnp.where(odd, rows[k + 1], rows[k]) for k in range(0, len(rows), 2)]
    return rows[0]


def three_parts(value):
    high, rest = two_parts(value)
    return high, rest, ((value - high) - rest).astype(jnp.bfloat16).astype(jnp.float32)


def two_parts(value):
    high = value.astype(jnp.bfloat16).astype(jnp.float32)
    return high, (value - high).astype(jnp.bfloat16).astype(jnp.float32)


def relative(p):
    return (p & 16) | ((p & 8) >> 1) | ((p & 4) << 1) | (p & 3)


def sums_kernel(
    slabs, owners,
    state_hbm, nbr_hbm, send_hbm, area_hbm, volume_hbm, left_hbm, right_hbm,
    out,
    state, nbr, send, area, volume, left, right,
    idx, areas, halo_idx, up, down, from_low, from_high, table_rows, table, factors, weights,
    own, near, work, outbox, inbox,
    in_sem, halo_send_sem, halo_recv_sem, send_sem, recv_sem, round_sem,
):
    space = lax.axis_index("space")
    inst = lax.axis_index("inst")
    has_above = space < slabs - 1
    has_below = space > 0
    above = lax.rem(space + 1, slabs)
    below = lax.rem(space + slabs - 1, slabs)
    f32 = jnp.float32
    bf16 = jnp.bfloat16

    loads = [
        pltpu.make_async_copy(src, dst, in_sem.at[k])
        for k, (src, dst) in enumerate(
            [
                (send_hbm, send), (state_hbm, state), (left_hbm, left), (right_hbm, right),
                (nbr_hbm, nbr), (area_hbm, area), (volume_hbm, volume),
            ]
        )
    ]
    for load in loads:
        load.start()

    barrier = pltpu.get_barrier_semaphore()

    @pl.when(has_above)
    def _():
        pl.semaphore_signal(barrier, inc=1, device_id={"space": above}, device_id_type=pl.DeviceIdType.MESH)

    @pl.when(has_below)
    def _():
        pl.semaphore_signal(barrier, inc=1, device_id={"space": below}, device_id_type=pl.DeviceIdType.MESH)

    for partner in (16, 6, 7, 4, 5, 8, 24, 2, 3, 1):
        pl.semaphore_signal(barrier, inc=1, device_id={"inst": inst ^ partner}, device_id_type=pl.DeviceIdType.MESH)

    loads[0].wait()
    loads[1].wait()
    for k in range(4):
        halo_idx[pl.ds(k, 1)] = send[0:1, LANES * k : LANES * (k + 1)]
        halo_idx[pl.ds(4 + k, 1)] = send[1:2, LANES * k : LANES * (k + 1)]
    hidx = halo_idx[...]
    hlane = hidx & (LANES - 1)
    hrow = (hidx >> 7) & 3
    upper = lax.broadcasted_iota(jnp.int32, (8, LANES), 0) < 4
    for c in range(NVAR):
        found = jnp.zeros((8, LANES), f32)
        for q in range(4):
            rows = jnp.where(upper, wide(state[c, pl.ds(28 + q, 1)]), wide(state[c, pl.ds(q, 1)]))
            found = jnp.where(hrow == q, lane_gather(rows, hlane), found)
        up[pl.ds(4 * c, 4)] = found[0:4]
        down[pl.ds(4 * c, 4)] = found[4:8]

    def prepare():
        loads[5].wait()
        loads[2].wait()
        loads[3].wait()
        factors[...] = jnp.zeros_like(factors)
        factors[0:NVAR, 0:NVAR] = left[...]
        factors[8 : 8 + NVAR, 0:NVAR] = right[...]
        eye = (
            lax.broadcasted_iota(jnp.int32, (8, LANES), 0) == lax.broadcasted_iota(jnp.int32, (8, LANES), 1)
        ).astype(f32)
        turned = lax.dot_general(
            eye, jnp.concatenate([factors[8:16], jnp.zeros((120, LANES), f32)], axis=0),
            (((1,), (1,)), ((), ())), precision=lax.Precision.HIGHEST, preferred_element_type=f32,
        )
        lane_at = lax.broadcasted_iota(jnp.int32, (8, LANES), 1)
        row_at = lax.broadcasted_iota(jnp.int32, (8, LANES), 0)
        for j in range(NVAR):
            line = factors[0:8] * wide(turned[j : j + 1])
            line = jnp.where((lane_at == NVAR) & (row_at == j), 1.0, line)
            high, rest, last = three_parts(line)
            packed = high + pltpu.roll(high, 8, 1) + pltpu.roll(rest, 16, 1) + pltpu.roll(rest, 24, 1)
            packed = packed + pltpu.roll(high, 32, 1) + pltpu.roll(last, 40, 1)
            weights[8 * j : 8 * j + 8] = packed.astype(bf16)

        for c in range(NVAR):
            table_rows[pl.ds(c, 32, stride=8)] = state[c]
        table_rows[pl.ds(NVAR, 32, stride=8)] = jnp.zeros((32, LANES), f32)
        high, rest = two_parts(table_rows[...])
        table[:, 0:LANES] = high.astype(bf16)
        table[:, LANES : 2 * LANES] = rest.astype(bf16)

        loads[4].wait()

        for p in range(32):
            q, k = p // 8, p % 8
            block = inst ^ relative(p)
            col = pl.multiple_of(block * LANES, LANES)
            idx[pl.ds(q * 48 + k, FACES, stride=8)] = nbr[:, pl.ds(col, LANES)]
            for x in range(3):
                areas[x, pl.ds(q * 48 + k, FACES, stride=8)] = area[x, :, pl.ds(col, LANES)]
            for c in range(NVAR):
                own[c, pl.ds(p, 1)] = state[c, pl.ds(block, 1)]

    def by_lanes(g):
        cells = idx[pl.ds(pl.multiple_of(g * 8, 8), 8)]
        lane = cells & (LANES - 1)
        row = cells >> 7
        found = [jnp.zeros((8, LANES), f32) for _ in range(NVAR)]
        for r in range(32):
            here = row == r
            for c in range(NVAR):
                found[c] = jnp.where(here, lane_gather(wide(state[c, pl.ds(r, 1)]), lane), found[c])
        for c in range(NVAR):
            near[pl.ds(g * 64 + c, 8, stride=8)] = found[c]

    position = lax.broadcasted_iota(jnp.int32, (LANES, LANES), 0).astype(f32).astype(bf16)

    def by_matrix(g):
        lines = [idx[pl.ds(g * 8 + a, 1)] for a in range(8)]
        chosen = []
        for line in lines:
            lane = jnp.broadcast_to((line & (LANES - 1)).astype(f32).astype(bf16), (LANES, LANES))
            one = jnp.where(position == lane, bf16(1), bf16(0))
            chosen.append(jnp.concatenate([one, one], axis=0))
        picked = jnp.dot(table[...], jnp.concatenate(chosen, axis=1), preferred_element_type=f32)
        for a in range(8):
            rows = [picked[8 * r : 8 * r + 8, LANES * a : LANES * (a + 1)] for r in range(32)]
            near[pl.ds(pl.multiple_of((g * 8 + a) * 8, 8), 8)] = bits_select(rows, wide(lines[a] >> 7), 5)

    def local(h, carry):
        for d in range(2 * FACES):
            if d in (0, 2, 5, 7, 10):
                by_lanes(h * 2 * FACES + d)
            else:
                by_matrix(h * 2 * FACES + d)
        return carry

    pl.semaphore_wait(barrier, 10 + has_above.astype(jnp.int32) + has_below.astype(jnp.int32))
    rise = pltpu.make_async_remote_copy(
        src_ref=up, dst_ref=from_low, send_sem=halo_send_sem.at[0], recv_sem=halo_recv_sem.at[0],
        device_id={"space": above}, device_id_type=pl.DeviceIdType.MESH,
    )
    sink = pltpu.make_async_remote_copy(
        src_ref=down, dst_ref=from_high, send_sem=halo_send_sem.at[1], recv_sem=halo_recv_sem.at[1],
        device_id={"space": below}, device_id_type=pl.DeviceIdType.MESH,
    )

    @pl.when(has_above)
    def _():
        rise.start()

    @pl.when(has_below)
    def _():
        sink.start()

    for partner in (16, 8, 24):
        pl.semaphore_signal(round_sem, inc=1, device_id={"inst": inst ^ partner}, device_id_type=pl.DeviceIdType.MESH)

    prepare()
    lax.fori_loop(0, 2, local, 0)


    @pl.when(has_below)
    def _():
        rise.wait_recv()

    @pl.when(has_above)
    def _():
        sink.wait_recv()

    @pl.when(space == 0)
    def _():
        from_low[...] = jnp.zeros_like(from_low)

    @pl.when(space == slabs - 1)
    def _():
        from_high[...] = jnp.zeros_like(from_high)

    def group(q, opening):
        first = q * 8
        totals = [jnp.zeros((8, LANES), f32) for _ in range(8)]
        for d in range(FACES):
            g = q * FACES + d
            at = g * 8
            cells = idx[pl.ds(at, 8)]
            lane = cells & (LANES - 1)
            row = cells >> 7
            found = [near[pl.ds(g * 64 + c, 8, stride=8)] for c in range(NVAR)]
            for r in range(8):
                here = row == 32 + r
                source = from_low if r < 4 else from_high
                for c in range(NVAR):
                    line = source[pl.ds(4 * c + r % 4, 1)]
                    found[c] = jnp.where(here, lane_gather(wide(line), lane), found[c])
            mean = [0.5 * (own[c, first : first + 8] + found[c]) for c in range(NVAR)]
            flux = (
                mean[1] * areas[0, pl.ds(at, 8)]
                + mean[2] * areas[1, pl.ds(at, 8)]
                + mean[3] * areas[2, pl.ds(at, 8)]
            )
            for c in range(8):
                work[d, pl.ds(c, 8, stride=8)] = mean[c] if c < NVAR else flux
            columns = []
            for a in range(8):
                high, rest = two_parts(work[d, 8 * a : 8 * a + 8])
                columns.append(jnp.concatenate([high, rest, high, rest], axis=0).astype(bf16))
            entries = jnp.dot(weights[:, 0:32], jnp.concatenate(columns, axis=1), preferred_element_type=f32)
            for a in range(8):
                row_sum = None
                for j in range(NVAR):
                    entry = jnp.abs(entries[8 * j : 8 * j + 8, LANES * a : LANES * (a + 1)])
                    row_sum = entry if row_sum is None else row_sum + entry
                work[d, 8 * a : 8 * a + 8] = row_sum
            largest = work[d, pl.ds(0, 8, stride=8)]
            for i in range(1, NVAR):
                largest = jnp.maximum(largest, work[d, pl.ds(i, 8, stride=8)])
            last = flux + (largest + 0.5)
            totals = [t + x for t, x in zip(totals, mean + [last])]
        for c in range(8):
            outbox[pl.ds(q * 64 + c, 8, stride=8)] = totals[c]

        if opening:
            pl.semaphore_wait(round_sem, 3)
        for p in range(first + 7, max(first, 1) - 1, -1):
            rel = relative(p)
            pltpu.make_async_remote_copy(
                src_ref=outbox.at[pl.ds(8 * p, 8)], dst_ref=inbox.at[pl.ds(8 * (rel - 1), 8)],
                send_sem=send_sem, recv_sem=recv_sem,
                device_id={"inst": inst ^ rel}, device_id_type=pl.DeviceIdType.MESH,
            ).start()

    for q in (3, 2, 1, 0):
        group(q, q == 3)
    pltpu.make_async_copy(inbox, inbox, recv_sem).wait()
    total = outbox[0:8]
    for k in range(31):
        total = total + inbox[8 * k : 8 * k + 8]
    high, rest, last = three_parts(total)
    parts = jnp.concatenate([high, rest, high, rest, last, high], axis=0).astype(bf16)
    out[0:56] = jnp.dot(weights[:, 0:48], parts, preferred_element_type=f32) * (0.5 / (FACES * INSTANCES))
    loads[6].wait()
    out[56:64] = frequency * wide(volume[...])
    pltpu.make_async_copy(inbox, inbox, send_sem).wait()

    @pl.when(has_above)
    def _():
        rise.wait_send()

    @pl.when(has_below)
    def _():
        sink.wait_send()


def invert_kernel(mean, out):
    harmonic = lax.broadcasted_iota(jnp.int32, (HARM, LANES), 0).astype(jnp.float32) + 1.0
    shift = harmonic * jnp.broadcast_to(mean[pl.ds(56, 1)], (HARM, LANES))
    real = {}
    imag = {}
    for i in range(NVAR):
        for j in range(NVAR):
            real[i, j] = jnp.broadcast_to(mean[pl.ds(8 * j + i, 1)], (HARM, LANES))
            imag[i, j] = shift if i == j else None

    def product(ar, ai, br, bi):
        if ai is None and bi is None:
            return ar * br, None
        if ai is None:
            return ar * br, ar * bi
        if bi is None:
            return ar * br, ai * br
        return ar * br - ai * bi, ar * bi + ai * br

    for k in range(NVAR):
        pr, pi = real[k, k], imag[k, k]
        norm = 1.0 / (pr * pr + pi * pi)
        pr, pi = pr * norm, -pi * norm
        for j in range(NVAR):
            if j != k:
                real[k, j], imag[k, j] = product(real[k, j], imag[k, j], pr, pi)
        real[k, k], imag[k, k] = pr, pi
        for i in range(NVAR):
            if i == k:
                continue
            fr, fi = real[i, k], imag[i, k]
            for j in range(NVAR):
                if j == k:
                    continue
                xr, xi = product(fr, fi, real[k, j], imag[k, j])
                real[i, j] = real[i, j] - xr
                if xi is not None:
                    imag[i, j] = -xi if imag[i, j] is None else imag[i, j] - xi
            xr, xi = product(fr, fi, pr, pi)
            real[i, k], imag[i, k] = -xr, -xi
    for i in range(NVAR):
        for j in range(NVAR):
            out[0, i, j] = real[i, j]
            out[1, i, j] = imag[i, j]


def per_device(flow_state, face_nbr, halo_send, face_area, cell_volume, flux_left, flux_right):
    slabs = lax.axis_size("space")
    owners = lax.axis_size("inst")
    share = cell_volume.shape[0]
    state = flow_state.reshape(NVAR, 32, LANES)
    vmem = pl.BlockSpec(memory_space=pltpu.VMEM)
    f32 = jnp.float32
    mean = pl.pallas_call(
        functools.partial(sums_kernel, slabs, owners),
        out_shape=jax.ShapeDtypeStruct((64, LANES), f32),
        in_specs=[pl.BlockSpec(memory_space=pltpu.HBM)] * 7,
        out_specs=vmem,
        scratch_shapes=[
            pltpu.VMEM((NVAR, 32, LANES), f32),
            pltpu.VMEM(face_nbr.shape, jnp.int32),
            pltpu.VMEM(halo_send.shape, jnp.int32),
            pltpu.VMEM(face_area.shape, f32),
            pltpu.VMEM((1, share), f32),
            pltpu.VMEM((NVAR, NVAR), f32),
            pltpu.VMEM((NVAR, NVAR), f32),
            pltpu.VMEM((192, LANES), jnp.int32),
            pltpu.VMEM((3, 192, LANES), f32),
            pltpu.VMEM((8, LANES), jnp.int32),
            pltpu.VMEM((28, LANES), f32),
            pltpu.VMEM((28, LANES), f32),
            pltpu.VMEM((28, LANES), f32),
            pltpu.VMEM((28, LANES), f32),
            pltpu.VMEM((256, LANES), f32),
            pltpu.VMEM((256, 2 * LANES), jnp.bfloat16),
            pltpu.VMEM((16, LANES), f32),
            pltpu.VMEM((56, LANES), jnp.bfloat16),
            pltpu.VMEM((NVAR, 32, LANES), f32),
            pltpu.VMEM((1536, LANES), f32),
            pltpu.VMEM((FACES, 64, LANES), f32),
            pltpu.VMEM((256, LANES), f32),
            pltpu.VMEM((248, LANES), f32),
            pltpu.SemaphoreType.DMA((7,)),
            pltpu.SemaphoreType.DMA((2,)),
            pltpu.SemaphoreType.DMA((2,)),
            pltpu.SemaphoreType.DMA,
            pltpu.SemaphoreType.DMA,
            pltpu.SemaphoreType.REGULAR,
        ],
        compiler_params=pltpu.CompilerParams(collective_id=0, has_side_effects=True, vmem_limit_bytes=24 << 20),
        name="sums",
    )(*[
        pltpu.with_memory_space_constraint(x, pltpu.HBM)
        for x in (state, face_nbr, halo_send, face_area, cell_volume.reshape(1, share), flux_left, flux_right)
    ])
    return pl.pallas_call(
        invert_kernel,
        out_shape=jax.ShapeDtypeStruct((2, NVAR, NVAR, HARM, share), f32),
        in_specs=[vmem],
        out_specs=vmem,
        compiler_params=pltpu.CompilerParams(vmem_limit_bytes=8 << 20),
        name="invert",
    )(mean)


def solution(mesh):
    placed = (
        P("inst", None, "space"),
        P(None, "space"),
        P(None, "space"),
        P(None, None, "space"),
        P(("space", "inst")),
        P(),
        P(),
    )
    return jax.shard_map(
        per_device,
        mesh=mesh,
        in_specs=placed,
        out_specs=P(None, None, None, None, ("space", "inst")),
        check_vma=False,
    )
```

```python
import functools

import jax
import jax.numpy as jnp
from jax import lax
from jax.experimental import pallas as pl
from jax.experimental.pallas import tpu as pltpu
from jax.sharding import PartitionSpec as P

INSTANCES = 32
HARM = 16
NVAR = 7
FACES = 6
LANES = 128

frequency = 0.1


def lane_gather(rows, lane):
    return jnp.take_along_axis(rows, lane, axis=1, mode="promise_in_bounds")


def wide(row):
    return jnp.broadcast_to(row, (8, LANES))


def bits_select(rows, index, bits):
    for b in range(bits):
        odd = ((index >> b) & 1) == 1
        rows = [jnp.where(odd, rows[k + 1], rows[k]) for k in range(0, len(rows), 2)]
    return rows[0]


def three_parts(value):
    high, rest = two_parts(value)
    return high, rest, ((value - high) - rest).astype(jnp.bfloat16).astype(jnp.float32)


def two_parts(value):
    high = value.astype(jnp.bfloat16).astype(jnp.float32)
    return high, (value - high).astype(jnp.bfloat16).astype(jnp.float32)


def relative(p):
    return (p & 16) | ((p & 8) >> 1) | ((p & 4) << 1) | (p & 3)


def sums_kernel(
    slabs, owners,
    state_hbm, nbr_hbm, send_hbm, area_hbm, volume_hbm, left_hbm, right_hbm,
    out,
    state, nbr, send, area, volume, left, right,
    idx, areas, halo_idx, up, down, from_low, from_high, table_rows, table, factors, weights,
    own, near, work, outbox, inbox,
    in_sem, halo_send_sem, halo_recv_sem, send_sem, recv_sem, round_sem,
):
    space = lax.axis_index("space")
    inst = lax.axis_index("inst")
    has_above = space < slabs - 1
    has_below = space > 0
    above = lax.rem(space + 1, slabs)
    below = lax.rem(space + slabs - 1, slabs)
    f32 = jnp.float32
    bf16 = jnp.bfloat16

    loads = [
        pltpu.make_async_copy(src, dst, in_sem.at[k])
        for k, (src, dst) in enumerate(
            [
                (send_hbm, send), (state_hbm, state), (left_hbm, left), (right_hbm, right),
                (nbr_hbm, nbr), (area_hbm, area), (volume_hbm, volume),
            ]
        )
    ]
    for load in loads:
        load.start()

    barrier = pltpu.get_barrier_semaphore()

    @pl.when(has_above)
    def _():
        pl.semaphore_signal(barrier, inc=1, device_id={"space": above}, device_id_type=pl.DeviceIdType.MESH)

    @pl.when(has_below)
    def _():
        pl.semaphore_signal(barrier, inc=1, device_id={"space": below}, device_id_type=pl.DeviceIdType.MESH)

    for partner in (16, 6, 7, 4, 5, 8, 24, 2, 3, 1):
        pl.semaphore_signal(barrier, inc=1, device_id={"inst": inst ^ partner}, device_id_type=pl.DeviceIdType.MESH)

    loads[0].wait()
    loads[1].wait()
    for k in range(4):
        halo_idx[pl.ds(k, 1)] = send[0:1, LANES * k : LANES * (k + 1)]
        halo_idx[pl.ds(4 + k, 1)] = send[1:2, LANES * k : LANES * (k + 1)]
    hidx = halo_idx[...]
    hlane = hidx & (LANES - 1)
    hrow = (hidx >> 7) & 3
    upper = lax.broadcasted_iota(jnp.int32, (8, LANES), 0) < 4
    for c in range(NVAR):
        found = jnp.zeros((8, LANES), f32)
        for q in range(4):
            rows = jnp.where(upper, wide(state[c, pl.ds(28 + q, 1)]), wide(state[c, pl.ds(q, 1)]))
            found = jnp.where(hrow == q, lane_gather(rows, hlane), found)
        up[pl.ds(4 * c, 4)] = found[0:4]
        down[pl.ds(4 * c, 4)] = found[4:8]

    def prepare():
        loads[5].wait()
        loads[2].wait()
        loads[3].wait()
        factors[...] = jnp.zeros_like(factors)
        factors[0:NVAR, 0:NVAR] = left[...]
        factors[8 : 8 + NVAR, 0:NVAR] = right[...]
        eye = (
            lax.broadcasted_iota(jnp.int32, (8, LANES), 0) == lax.broadcasted_iota(jnp.int32, (8, LANES), 1)
        ).astype(f32)
        turned = lax.dot_general(
            eye, jnp.concatenate([factors[8:16], jnp.zeros((120, LANES), f32)], axis=0),
            (((1,), (1,)), ((), ())), precision=lax.Precision.HIGHEST, preferred_element_type=f32,
        )
        lane_at = lax.broadcasted_iota(jnp.int32, (8, LANES), 1)
        row_at = lax.broadcasted_iota(jnp.int32, (8, LANES), 0)
        for j in range(NVAR):
            line = factors[0:8] * wide(turned[j : j + 1])
            line = jnp.where((lane_at == NVAR) & (row_at == j), 1.0, line)
            high, rest, last = three_parts(line)
            packed = high + pltpu.roll(high, 8, 1) + pltpu.roll(rest, 16, 1) + pltpu.roll(rest, 24, 1)
            packed = packed + pltpu.roll(high, 32, 1) + pltpu.roll(last, 40, 1)
            weights[8 * j : 8 * j + 8] = packed.astype(bf16)

        for c in range(NVAR):
            table_rows[pl.ds(c, 32, stride=8)] = state[c]
        table_rows[pl.ds(NVAR, 32, stride=8)] = jnp.zeros((32, LANES), f32)
        high, rest = two_parts(table_rows[...])
        table[:, 0:LANES] = high.astype(bf16)
        table[:, LANES : 2 * LANES] = rest.astype(bf16)

        loads[4].wait()

        for p in range(32):
            q, k = p // 8, p % 8
            block = inst ^ relative(p)
            col = pl.multiple_of(block * LANES, LANES)
            idx[pl.ds(q * 48 + k, FACES, stride=8)] = nbr[:, pl.ds(col, LANES)]
            for x in range(3):
                areas[x, pl.ds(q * 48 + k, FACES, stride=8)] = area[x, :, pl.ds(col, LANES)]
            for c in range(NVAR):
                own[c, pl.ds(p, 1)] = state[c, pl.ds(block, 1)]

    def by_lanes(g):
        cells = idx[pl.ds(pl.multiple_of(g * 8, 8), 8)]
        lane = cells & (LANES - 1)
        row = cells >> 7
        found = [jnp.zeros((8, LANES), f32) for _ in range(NVAR)]
        for r in range(32):
            here = row == r
            for c in range(NVAR):
                found[c] = jnp.where(here, lane_gather(wide(state[c, pl.ds(r, 1)]), lane), found[c])
        for c in range(NVAR):
            near[pl.ds(g * 64 + c, 8, stride=8)] = found[c]

    position = lax.broadcasted_iota(jnp.int32, (LANES, LANES), 0).astype(f32).astype(bf16)

    def by_matrix(g):
        lines = [idx[pl.ds(g * 8 + a, 1)] for a in range(8)]
        chosen = []
        for line in lines:
            lane = jnp.broadcast_to((line & (LANES - 1)).astype(f32).astype(bf16), (LANES, LANES))
            one = jnp.where(position == lane, bf16(1), bf16(0))
            chosen.append(jnp.concatenate([one, one], axis=0))
        picked = jnp.dot(table[...], jnp.concatenate(chosen, axis=1), preferred_element_type=f32)
        for a in range(8):
            rows = [picked[8 * r : 8 * r + 8, LANES * a : LANES * (a + 1)] for r in range(32)]
            near[pl.ds(pl.multiple_of((g * 8 + a) * 8, 8), 8)] = bits_select(rows, wide(lines[a] >> 7), 5)

    def local(h, carry):
        for d in range(2 * FACES):
            if d in (0, 2, 5, 7, 10):
                by_lanes(h * 2 * FACES + d)
            else:
                by_matrix(h * 2 * FACES + d)
        return carry

    pl.semaphore_wait(barrier, 10 + has_above.astype(jnp.int32) + has_below.astype(jnp.int32))
    rise = pltpu.make_async_remote_copy(
        src_ref=up, dst_ref=from_low, send_sem=halo_send_sem.at[0], recv_sem=halo_recv_sem.at[0],
        device_id={"space": above}, device_id_type=pl.DeviceIdType.MESH,
    )
    sink = pltpu.make_async_remote_copy(
        src_ref=down, dst_ref=from_high, send_sem=halo_send_sem.at[1], recv_sem=halo_recv_sem.at[1],
        device_id={"space": below}, device_id_type=pl.DeviceIdType.MESH,
    )

    @pl.when(has_above)
    def _():
        rise.start()

    @pl.when(has_below)
    def _():
        sink.start()

    for partner in (16, 8, 24):
        pl.semaphore_signal(round_sem, inc=1, device_id={"inst": inst ^ partner}, device_id_type=pl.DeviceIdType.MESH)

    prepare()
    lax.fori_loop(0, 2, local, 0)


    @pl.when(has_below)
    def _():
        rise.wait_recv()

    @pl.when(has_above)
    def _():
        sink.wait_recv()

    @pl.when(space == 0)
    def _():
        from_low[...] = jnp.zeros_like(from_low)

    @pl.when(space == slabs - 1)
    def _():
        from_high[...] = jnp.zeros_like(from_high)

    def group(q, opening):
        first = q * 8
        totals = [jnp.zeros((8, LANES), f32) for _ in range(8)]
        for d in range(FACES):
            g = q * FACES + d
            at = g * 8
            cells = idx[pl.ds(at, 8)]
            lane = cells & (LANES - 1)
            row = cells >> 7
            found = [near[pl.ds(g * 64 + c, 8, stride=8)] for c in range(NVAR)]
            for r in range(8):
                here = row == 32 + r
                source = from_low if r < 4 else from_high
                for c in range(NVAR):
                    line = source[pl.ds(4 * c + r % 4, 1)]
                    found[c] = jnp.where(here, lane_gather(wide(line), lane), found[c])
            mean = [0.5 * (own[c, first : first + 8] + found[c]) for c in range(NVAR)]
            flux = (
                mean[1] * areas[0, pl.ds(at, 8)]
                + mean[2] * areas[1, pl.ds(at, 8)]
                + mean[3] * areas[2, pl.ds(at, 8)]
            )
            for c in range(8):
                work[d, pl.ds(c, 8, stride=8)] = mean[c] if c < NVAR else flux
            columns = []
            for a in range(8):
                high, rest = two_parts(work[d, 8 * a : 8 * a + 8])
                columns.append(jnp.concatenate([high, rest, high, rest], axis=0).astype(bf16))
            entries = jnp.dot(weights[:, 0:32], jnp.concatenate(columns, axis=1), preferred_element_type=f32)
            for a in range(8):
                row_sum = None
                for j in range(NVAR):
                    entry = jnp.abs(entries[8 * j : 8 * j + 8, LANES * a : LANES * (a + 1)])
                    row_sum = entry if row_sum is None else row_sum + entry
                work[d, 8 * a : 8 * a + 8] = row_sum
            largest = work[d, pl.ds(0, 8, stride=8)]
            for i in range(1, NVAR):
                largest = jnp.maximum(largest, work[d, pl.ds(i, 8, stride=8)])
            last = flux + (largest + 0.5)
            totals = [t + x for t, x in zip(totals, mean + [last])]
        for c in range(8):
            outbox[pl.ds(q * 64 + c, 8, stride=8)] = totals[c]

        if opening:
            pl.semaphore_wait(round_sem, 3)
        for p in range(first + 7, max(first, 1) - 1, -1):
            rel = relative(p)
            pltpu.make_async_remote_copy(
                src_ref=outbox.at[pl.ds(8 * p, 8)], dst_ref=inbox.at[pl.ds(8 * (rel - 1), 8)],
                send_sem=send_sem, recv_sem=recv_sem,
                device_id={"inst": inst ^ rel}, device_id_type=pl.DeviceIdType.MESH,
            ).start()

    for q in (3, 2, 1, 0):
        group(q, q == 3)
    pltpu.make_async_copy(inbox, inbox, recv_sem).wait()
    total = outbox[0:8]
    for k in range(31):
        total = total + inbox[8 * k : 8 * k + 8]
    high, rest, last = three_parts(total)
    parts = jnp.concatenate([high, rest, high, rest, last, high], axis=0).astype(bf16)
    out[0:56] = jnp.dot(weights[:, 0:48], parts, preferred_element_type=f32) * (0.5 / (FACES * INSTANCES))
    loads[6].wait()
    out[56:64] = frequency * wide(volume[...])
    pltpu.make_async_copy(inbox, inbox, send_sem).wait()

    @pl.when(has_above)
    def _():
        rise.wait_send()

    @pl.when(has_below)
    def _():
        sink.wait_send()


def invert_half(mean, half, ready):
    harmonic = lax.broadcasted_iota(jnp.int32, (8, LANES), 0).astype(jnp.float32) + (8.0 * half + 1.0)
    shift = harmonic * jnp.broadcast_to(mean[pl.ds(56, 1)], (8, LANES))
    real = {}
    imag = {}
    for i in range(NVAR):
        for j in range(NVAR):
            real[i, j] = jnp.broadcast_to(mean[pl.ds(8 * j + i, 1)], (8, LANES))
            imag[i, j] = shift if i == j else None

    def product(ar, ai, br, bi):
        if ai is None and bi is None:
            return ar * br, None
        if ai is None:
            return ar * br, ar * bi
        if bi is None:
            return ar * br, ai * br
        return ar * br - ai * bi, ar * bi + ai * br

    for k in range(NVAR):
        pr, pi = real[k, k], imag[k, k]
        norm = 1.0 / (pr * pr + pi * pi)
        pr, pi = pr * norm, -pi * norm
        for j in range(NVAR):
            if j != k:
                real[k, j], imag[k, j] = product(real[k, j], imag[k, j], pr, pi)
        real[k, k], imag[k, k] = pr, pi
        for i in range(NVAR):
            if i == k:
                continue
            fr, fi = real[i, k], imag[i, k]
            for j in range(NVAR):
                if j == k:
                    continue
                xr, xi = product(fr, fi, real[k, j], imag[k, j])
                real[i, j] = real[i, j] - xr
                if xi is not None:
                    imag[i, j] = -xi if imag[i, j] is None else imag[i, j] - xi
            xr, xi = product(fr, fi, pr, pi)
            real[i, k], imag[i, k] = -xr, -xi
    for i in range(NVAR):
        for j in range(NVAR):
            ready[half, 0, i, j] = real[i, j]
            ready[half, 1, i, j] = imag[i, j]


def invert_kernel(mean, out, ready, sem):
    copies = []
    for half in range(2):
        invert_half(mean, half, ready)
        copy = pltpu.make_async_copy(ready.at[half], out.at[:, :, :, pl.ds(8 * half, 8)], sem.at[half])
        copy.start()
        copies.append(copy)
    for copy in copies:
        copy.wait()


def per_device(flow_state, face_nbr, halo_send, face_area, cell_volume, flux_left, flux_right):
    slabs = lax.axis_size("space")
    owners = lax.axis_size("inst")
    share = cell_volume.shape[0]
    state = flow_state.reshape(NVAR, 32, LANES)
    vmem = pl.BlockSpec(memory_space=pltpu.VMEM)
    f32 = jnp.float32
    mean = pl.pallas_call(
        functools.partial(sums_kernel, slabs, owners),
        out_shape=jax.ShapeDtypeStruct((64, LANES), f32),
        in_specs=[pl.BlockSpec(memory_space=pltpu.HBM)] * 7,
        out_specs=vmem,
        scratch_shapes=[
            pltpu.VMEM((NVAR, 32, LANES), f32),
            pltpu.VMEM(face_nbr.shape, jnp.int32),
            pltpu.VMEM(halo_send.shape, jnp.int32),
            pltpu.VMEM(face_area.shape, f32),
            pltpu.VMEM((1, share), f32),
            pltpu.VMEM((NVAR, NVAR), f32),
            pltpu.VMEM((NVAR, NVAR), f32),
            pltpu.VMEM((192, LANES), jnp.int32),
            pltpu.VMEM((3, 192, LANES), f32),
            pltpu.VMEM((8, LANES), jnp.int32),
            pltpu.VMEM((28, LANES), f32),
            pltpu.VMEM((28, LANES), f32),
            pltpu.VMEM((28, LANES), f32),
            pltpu.VMEM((28, LANES), f32),
            pltpu.VMEM((256, LANES), f32),
            pltpu.VMEM((256, 2 * LANES), jnp.bfloat16),
            pltpu.VMEM((16, LANES), f32),
            pltpu.VMEM((56, LANES), jnp.bfloat16),
            pltpu.VMEM((NVAR, 32, LANES), f32),
            pltpu.VMEM((1536, LANES), f32),
            pltpu.VMEM((FACES, 64, LANES), f32),
            pltpu.VMEM((256, LANES), f32),
            pltpu.VMEM((248, LANES), f32),
            pltpu.SemaphoreType.DMA((7,)),
            pltpu.SemaphoreType.DMA((2,)),
            pltpu.SemaphoreType.DMA((2,)),
            pltpu.SemaphoreType.DMA,
            pltpu.SemaphoreType.DMA,
            pltpu.SemaphoreType.REGULAR,
        ],
        compiler_params=pltpu.CompilerParams(collective_id=0, has_side_effects=True, vmem_limit_bytes=24 << 20),
        name="sums",
    )(*[
        pltpu.with_memory_space_constraint(x, pltpu.HBM)
        for x in (state, face_nbr, halo_send, face_area, cell_volume.reshape(1, share), flux_left, flux_right)
    ])
    return pl.pallas_call(
        invert_kernel,
        out_shape=jax.ShapeDtypeStruct((2, NVAR, NVAR, HARM, share), f32),
        in_specs=[vmem],
        out_specs=pl.BlockSpec(memory_space=pltpu.HBM),
        scratch_shapes=[pltpu.VMEM((2, 2, NVAR, NVAR, 8, share), f32), pltpu.SemaphoreType.DMA((2,))],
        compiler_params=pltpu.CompilerParams(vmem_limit_bytes=8 << 20),
        name="invert",
    )(mean)


def solution(mesh):
    placed = (
        P("inst", None, "space"),
        P(None, "space"),
        P(None, "space"),
        P(None, None, "space"),
        P(("space", "inst")),
        P(),
        P(),
    )
    return jax.shard_map(
        per_device,
        mesh=mesh,
        in_specs=placed,
        out_specs=P(None, None, None, None, ("space", "inst")),
        check_vma=False,
    )
```

```python
import functools

import jax
import jax.numpy as jnp
from jax import lax
from jax.experimental import pallas as pl
from jax.experimental.pallas import tpu as pltpu
from jax.sharding import PartitionSpec as P

INSTANCES = 32
HARM = 16
NVAR = 7
FACES = 6
LANES = 128

frequency = 0.1


def lane_gather(rows, lane):
    return jnp.take_along_axis(rows, lane, axis=1, mode="promise_in_bounds")


def wide(row):
    return jnp.broadcast_to(row, (8, LANES))


def bits_select(rows, index, bits):
    for b in range(bits):
        odd = ((index >> b) & 1) == 1
        rows = [jnp.where(odd, rows[k + 1], rows[k]) for k in range(0, len(rows), 2)]
    return rows[0]


def three_parts(value):
    high, rest = two_parts(value)
    return high, rest, ((value - high) - rest).astype(jnp.bfloat16).astype(jnp.float32)


def two_parts(value):
    high = value.astype(jnp.bfloat16).astype(jnp.float32)
    return high, (value - high).astype(jnp.bfloat16).astype(jnp.float32)


def relative(p):
    return (p & 16) | ((p & 8) >> 1) | ((p & 4) << 1) | (p & 3)


def sums_kernel(
    slabs, owners,
    state_hbm, nbr_hbm, send_hbm, area_hbm, volume_hbm, left_hbm, right_hbm,
    out,
    state, nbr, send, area, volume, left, right,
    idx, areas, halo_idx, up, down, from_low, from_high, table_rows, table, factors, weights,
    own, near, work, outbox, inbox,
    in_sem, halo_send_sem, halo_recv_sem, send_sem, recv_sem, round_sem,
):
    space = lax.axis_index("space")
    inst = lax.axis_index("inst")
    has_above = space < slabs - 1
    has_below = space > 0
    above = lax.rem(space + 1, slabs)
    below = lax.rem(space + slabs - 1, slabs)
    f32 = jnp.float32
    bf16 = jnp.bfloat16

    loads = [
        pltpu.make_async_copy(src, dst, in_sem.at[k])
        for k, (src, dst) in enumerate(
            [
                (send_hbm, send), (state_hbm, state), (left_hbm, left), (right_hbm, right),
                (nbr_hbm, nbr), (area_hbm, area), (volume_hbm, volume),
            ]
        )
    ]
    for load in loads:
        load.start()

    barrier = pltpu.get_barrier_semaphore()

    @pl.when(has_above)
    def _():
        pl.semaphore_signal(barrier, inc=1, device_id={"space": above}, device_id_type=pl.DeviceIdType.MESH)

    @pl.when(has_below)
    def _():
        pl.semaphore_signal(barrier, inc=1, device_id={"space": below}, device_id_type=pl.DeviceIdType.MESH)

    for partner in (16, 6, 7, 4, 5, 8, 24, 2, 3, 1):
        pl.semaphore_signal(barrier, inc=1, device_id={"inst": inst ^ partner}, device_id_type=pl.DeviceIdType.MESH)

    loads[0].wait()
    loads[1].wait()
    for k in range(4):
        halo_idx[pl.ds(k, 1)] = send[0:1, LANES * k : LANES * (k + 1)]
        halo_idx[pl.ds(4 + k, 1)] = send[1:2, LANES * k : LANES * (k + 1)]
    hidx = halo_idx[...]
    hlane = hidx & (LANES - 1)
    hrow = (hidx >> 7) & 3
    upper = lax.broadcasted_iota(jnp.int32, (8, LANES), 0) < 4
    for c in range(NVAR):
        found = jnp.zeros((8, LANES), f32)
        for q in range(4):
            rows = jnp.where(upper, wide(state[c, pl.ds(28 + q, 1)]), wide(state[c, pl.ds(q, 1)]))
            found = jnp.where(hrow == q, lane_gather(rows, hlane), found)
        up[pl.ds(4 * c, 4)] = found[0:4]
        down[pl.ds(4 * c, 4)] = found[4:8]

    def prepare():
        loads[5].wait()
        loads[2].wait()
        loads[3].wait()
        factors[...] = jnp.zeros_like(factors)
        factors[0:NVAR, 0:NVAR] = left[...]
        factors[8 : 8 + NVAR, 0:NVAR] = right[...]
        eye = (
            lax.broadcasted_iota(jnp.int32, (8, LANES), 0) == lax.broadcasted_iota(jnp.int32, (8, LANES), 1)
        ).astype(f32)
        turned = lax.dot_general(
            eye, jnp.concatenate([factors[8:16], jnp.zeros((120, LANES), f32)], axis=0),
            (((1,), (1,)), ((), ())), precision=lax.Precision.HIGHEST, preferred_element_type=f32,
        )
        lane_at = lax.broadcasted_iota(jnp.int32, (8, LANES), 1)
        row_at = lax.broadcasted_iota(jnp.int32, (8, LANES), 0)
        for j in range(NVAR):
            line = factors[0:8] * wide(turned[j : j + 1])
            line = jnp.where((lane_at == NVAR) & (row_at == j), 1.0, line)
            high, rest, last = three_parts(line)
            packed = high + pltpu.roll(high, 8, 1) + pltpu.roll(rest, 16, 1) + pltpu.roll(rest, 24, 1)
            packed = packed + pltpu.roll(high, 32, 1) + pltpu.roll(last, 40, 1)
            weights[8 * j : 8 * j + 8] = packed.astype(bf16)

        for c in range(NVAR):
            table_rows[pl.ds(c, 32, stride=8)] = state[c]
        table_rows[pl.ds(NVAR, 32, stride=8)] = jnp.zeros((32, LANES), f32)
        high, rest = two_parts(table_rows[...])
        table[:, 0:LANES] = high.astype(bf16)
        table[:, LANES : 2 * LANES] = rest.astype(bf16)

        loads[4].wait()

        for p in range(32):
            q, k = p // 8, p % 8
            block = inst ^ relative(p)
            col = pl.multiple_of(block * LANES, LANES)
            idx[pl.ds(q * 48 + k, FACES, stride=8)] = nbr[:, pl.ds(col, LANES)]
            for x in range(3):
                areas[x, pl.ds(q * 48 + k, FACES, stride=8)] = area[x, :, pl.ds(col, LANES)]
            for c in range(NVAR):
                own[c, pl.ds(p, 1)] = state[c, pl.ds(block, 1)]

    def by_lanes(g):
        cells = idx[pl.ds(pl.multiple_of(g * 8, 8), 8)]
        lane = cells & (LANES - 1)
        row = cells >> 7
        found = [jnp.zeros((8, LANES), f32) for _ in range(NVAR)]
        for r in range(32):
            here = row == r
            for c in range(NVAR):
                found[c] = jnp.where(here, lane_gather(wide(state[c, pl.ds(r, 1)]), lane), found[c])
        for c in range(NVAR):
            near[pl.ds(g * 64 + c, 8, stride=8)] = found[c]

    position = lax.broadcasted_iota(jnp.int32, (LANES, LANES), 0).astype(f32).astype(bf16)

    def by_matrix(g):
        lines = [idx[pl.ds(g * 8 + a, 1)] for a in range(8)]
        chosen = []
        for line in lines:
            lane = jnp.broadcast_to((line & (LANES - 1)).astype(f32).astype(bf16), (LANES, LANES))
            one = jnp.where(position == lane, bf16(1), bf16(0))
            chosen.append(jnp.concatenate([one, one], axis=0))
        picked = jnp.dot(table[...], jnp.concatenate(chosen, axis=1), preferred_element_type=f32)
        for a in range(8):
            rows = [picked[8 * r : 8 * r + 8, LANES * a : LANES * (a + 1)] for r in range(32)]
            near[pl.ds(pl.multiple_of((g * 8 + a) * 8, 8), 8)] = bits_select(rows, wide(lines[a] >> 7), 5)

    def local(h, carry):
        for d in range(2 * FACES):
            if d in (0, 2, 5, 7, 10):
                by_lanes(h * 2 * FACES + d)
            else:
                by_matrix(h * 2 * FACES + d)
        return carry

    pl.semaphore_wait(barrier, 10 + has_above.astype(jnp.int32) + has_below.astype(jnp.int32))
    rise = pltpu.make_async_remote_copy(
        src_ref=up, dst_ref=from_low, send_sem=halo_send_sem.at[0], recv_sem=halo_recv_sem.at[0],
        device_id={"space": above}, device_id_type=pl.DeviceIdType.MESH,
    )
    sink = pltpu.make_async_remote_copy(
        src_ref=down, dst_ref=from_high, send_sem=halo_send_sem.at[1], recv_sem=halo_recv_sem.at[1],
        device_id={"space": below}, device_id_type=pl.DeviceIdType.MESH,
    )

    @pl.when(has_above)
    def _():
        rise.start()

    @pl.when(has_below)
    def _():
        sink.start()

    for partner in (16, 8, 24):
        pl.semaphore_signal(round_sem, inc=1, device_id={"inst": inst ^ partner}, device_id_type=pl.DeviceIdType.MESH)

    prepare()
    lax.fori_loop(0, 2, local, 0)


    @pl.when(has_below)
    def _():
        rise.wait_recv()

    @pl.when(has_above)
    def _():
        sink.wait_recv()

    @pl.when(space == 0)
    def _():
        from_low[...] = jnp.zeros_like(from_low)

    @pl.when(space == slabs - 1)
    def _():
        from_high[...] = jnp.zeros_like(from_high)

    def group(q, opening):
        first = q * 8
        totals = [jnp.zeros((8, LANES), f32) for _ in range(8)]
        for d in range(FACES):
            g = q * FACES + d
            at = g * 8
            cells = idx[pl.ds(at, 8)]
            lane = cells & (LANES - 1)
            row = cells >> 7
            found = [near[pl.ds(g * 64 + c, 8, stride=8)] for c in range(NVAR)]
            for r in range(8):
                here = row == 32 + r
                source = from_low if r < 4 else from_high
                for c in range(NVAR):
                    line = source[pl.ds(4 * c + r % 4, 1)]
                    found[c] = jnp.where(here, lane_gather(wide(line), lane), found[c])
            mean = [0.5 * (own[c, first : first + 8] + found[c]) for c in range(NVAR)]
            flux = (
                mean[1] * areas[0, pl.ds(at, 8)]
                + mean[2] * areas[1, pl.ds(at, 8)]
                + mean[3] * areas[2, pl.ds(at, 8)]
            )
            for c in range(8):
                work[d, pl.ds(c, 8, stride=8)] = mean[c] if c < NVAR else flux
            columns = []
            for a in range(8):
                high, rest = two_parts(work[d, 8 * a : 8 * a + 8])
                columns.append(jnp.concatenate([high, rest, high, rest], axis=0).astype(bf16))
            entries = jnp.dot(weights[:, 0:32], jnp.concatenate(columns, axis=1), preferred_element_type=f32)
            for a in range(8):
                row_sum = None
                for j in range(NVAR):
                    entry = jnp.abs(entries[8 * j : 8 * j + 8, LANES * a : LANES * (a + 1)])
                    row_sum = entry if row_sum is None else row_sum + entry
                work[d, 8 * a : 8 * a + 8] = row_sum
            largest = work[d, pl.ds(0, 8, stride=8)]
            for i in range(1, NVAR):
                largest = jnp.maximum(largest, work[d, pl.ds(i, 8, stride=8)])
            last = flux + (largest + 0.5)
            totals = [t + x for t, x in zip(totals, mean + [last])]
        for c in range(8):
            outbox[pl.ds(q * 64 + c, 8, stride=8)] = totals[c]

        if opening:
            pl.semaphore_wait(round_sem, 3)
        for p in range(first + 7, max(first, 1) - 1, -1):
            rel = relative(p)
            pltpu.make_async_remote_copy(
                src_ref=outbox.at[pl.ds(8 * p, 8)], dst_ref=inbox.at[pl.ds(8 * (rel - 1), 8)],
                send_sem=send_sem, recv_sem=recv_sem,
                device_id={"inst": inst ^ rel}, device_id_type=pl.DeviceIdType.MESH,
            ).start()

    for q in (3, 2, 1, 0):
        group(q, q == 3)
    loads[6].wait()
    out[56:64] = frequency * wide(volume[...])
    pltpu.make_async_copy(inbox, inbox, recv_sem).wait()
    terms = [outbox[0:8]] + [inbox[8 * k : 8 * k + 8] for k in range(31)]
    while len(terms) > 1:
        terms = [a + b for a, b in zip(terms[::2], terms[1::2])]
    total = terms[0]
    high, rest, last = three_parts(total)
    parts = jnp.concatenate([high, rest, high, rest, last, high], axis=0).astype(bf16)
    out[0:56] = jnp.dot(weights[:, 0:48], parts, preferred_element_type=f32) * (0.5 / (FACES * INSTANCES))
    pltpu.make_async_copy(inbox, inbox, send_sem).wait()

    @pl.when(has_above)
    def _():
        rise.wait_send()

    @pl.when(has_below)
    def _():
        sink.wait_send()


def invert_half(mean, half, ready):
    harmonic = lax.broadcasted_iota(jnp.int32, (8, LANES), 0).astype(jnp.float32) + (8.0 * half + 1.0)
    shift = harmonic * jnp.broadcast_to(mean[pl.ds(56, 1)], (8, LANES))
    real = {}
    imag = {}
    for i in range(NVAR):
        for j in range(NVAR):
            real[i, j] = jnp.broadcast_to(mean[pl.ds(8 * j + i, 1)], (8, LANES))
            imag[i, j] = shift if i == j else None

    def product(ar, ai, br, bi):
        if ai is None and bi is None:
            return ar * br, None
        if ai is None:
            return ar * br, ar * bi
        if bi is None:
            return ar * br, ai * br
        return ar * br - ai * bi, ar * bi + ai * br

    for k in range(NVAR):
        pr, pi = real[k, k], imag[k, k]
        norm = 1.0 / (pr * pr + pi * pi)
        pr, pi = pr * norm, -pi * norm
        for j in range(NVAR):
            if j != k:
                real[k, j], imag[k, j] = product(real[k, j], imag[k, j], pr, pi)
        real[k, k], imag[k, k] = pr, pi
        for i in range(NVAR):
            if i == k:
                continue
            fr, fi = real[i, k], imag[i, k]
            for j in range(NVAR):
                if j == k:
                    continue
                xr, xi = product(fr, fi, real[k, j], imag[k, j])
                real[i, j] = real[i, j] - xr
                if xi is not None:
                    imag[i, j] = -xi if imag[i, j] is None else imag[i, j] - xi
            xr, xi = product(fr, fi, pr, pi)
            real[i, k], imag[i, k] = -xr, -xi
    for i in range(NVAR):
        for j in range(NVAR):
            ready[half, 0, i, j] = real[i, j]
            ready[half, 1, i, j] = imag[i, j]


def invert_kernel(mean, out, ready, sem):
    copies = []
    for half in range(2):
        invert_half(mean, half, ready)
        copy = pltpu.make_async_copy(ready.at[half], out.at[:, :, :, pl.ds(8 * half, 8)], sem.at[half])
        copy.start()
        copies.append(copy)
    for copy in copies:
        copy.wait()


def per_device(flow_state, face_nbr, halo_send, face_area, cell_volume, flux_left, flux_right):
    slabs = lax.axis_size("space")
    owners = lax.axis_size("inst")
    share = cell_volume.shape[0]
    state = flow_state.reshape(NVAR, 32, LANES)
    vmem = pl.BlockSpec(memory_space=pltpu.VMEM)
    f32 = jnp.float32
    mean = pl.pallas_call(
        functools.partial(sums_kernel, slabs, owners),
        out_shape=jax.ShapeDtypeStruct((64, LANES), f32),
        in_specs=[pl.BlockSpec(memory_space=pltpu.HBM)] * 7,
        out_specs=vmem,
        scratch_shapes=[
            pltpu.VMEM((NVAR, 32, LANES), f32),
            pltpu.VMEM(face_nbr.shape, jnp.int32),
            pltpu.VMEM(halo_send.shape, jnp.int32),
            pltpu.VMEM(face_area.shape, f32),
            pltpu.VMEM((1, share), f32),
            pltpu.VMEM((NVAR, NVAR), f32),
            pltpu.VMEM((NVAR, NVAR), f32),
            pltpu.VMEM((192, LANES), jnp.int32),
            pltpu.VMEM((3, 192, LANES), f32),
            pltpu.VMEM((8, LANES), jnp.int32),
            pltpu.VMEM((28, LANES), f32),
            pltpu.VMEM((28, LANES), f32),
            pltpu.VMEM((28, LANES), f32),
            pltpu.VMEM((28, LANES), f32),
            pltpu.VMEM((256, LANES), f32),
            pltpu.VMEM((256, 2 * LANES), jnp.bfloat16),
            pltpu.VMEM((16, LANES), f32),
            pltpu.VMEM((56, LANES), jnp.bfloat16),
            pltpu.VMEM((NVAR, 32, LANES), f32),
            pltpu.VMEM((1536, LANES), f32),
            pltpu.VMEM((FACES, 64, LANES), f32),
            pltpu.VMEM((256, LANES), f32),
            pltpu.VMEM((248, LANES), f32),
            pltpu.SemaphoreType.DMA((7,)),
            pltpu.SemaphoreType.DMA((2,)),
            pltpu.SemaphoreType.DMA((2,)),
            pltpu.SemaphoreType.DMA,
            pltpu.SemaphoreType.DMA,
            pltpu.SemaphoreType.REGULAR,
        ],
        compiler_params=pltpu.CompilerParams(collective_id=0, has_side_effects=True, vmem_limit_bytes=24 << 20),
        name="sums",
    )(*[
        pltpu.with_memory_space_constraint(x, pltpu.HBM)
        for x in (state, face_nbr, halo_send, face_area, cell_volume.reshape(1, share), flux_left, flux_right)
    ])
    return pl.pallas_call(
        invert_kernel,
        out_shape=jax.ShapeDtypeStruct((2, NVAR, NVAR, HARM, share), f32),
        in_specs=[vmem],
        out_specs=pl.BlockSpec(memory_space=pltpu.HBM),
        scratch_shapes=[pltpu.VMEM((2, 2, NVAR, NVAR, 8, share), f32), pltpu.SemaphoreType.DMA((2,))],
        compiler_params=pltpu.CompilerParams(vmem_limit_bytes=8 << 20),
        name="invert",
    )(mean)


def solution(mesh):
    placed = (
        P("inst", None, "space"),
        P(None, "space"),
        P(None, "space"),
        P(None, None, "space"),
        P(("space", "inst")),
        P(),
        P(),
    )
    return jax.shard_map(
        per_device,
        mesh=mesh,
        in_specs=placed,
        out_specs=P(None, None, None, None, ("space", "inst")),
        check_vma=False,
    )
```
